32 devices in a mesh: section: 4 (over y, core), chan: 8 (over z, x).
Axes of the slice: x: 2, y: 2, z: 4, core: 2. Of those that a mesh axis runs over, the one named last changes fastest.
Arguments:
- raw_traces: bfloat16 [2048, 1024], P(('section', 'chan')), may hold values from -6 to 6
- fir_taps: bfloat16 [64], replicated, may hold values from -0.75 to 0.75
- space_taps: float32 [33], replicated, may hold values from -1 to 1
- source_index: int32 [4, 96], P('section', 'chan'), may hold values from 0 to 511, as said below
Outputs:
- gathers: bfloat16 [2048, 64, 96], P(('section', 'chan'))
The draws below stay inside these ranges and needn't reach their ends.
Inputs may be any that keep to these rules, and one draw needn't show every extreme that they name: `source_index`: entries j * 12 to (j + 1) * 12 - 1 of a section's row are distinct and lie in channels j * 64 to (j + 1) * 64 - 1; the first such block of every section names channel 0 and the last names channel 512 - 1.
All inputs are finite; a program needn't handle non-finite values.
Results may differ from the reference program's by a relative error of at most 0.0058.
Values may be sent and summed in bfloat16 or wider, within the bound.
A program may use at most 64 MiB of HBM per device.

```python
import jax
import jax.numpy as jnp
from jax import lax

CH_DEV = 64
NT = 1024
KT = 64
SK = 33
LAGS = 64
SRC_DEV = 12
SRC = 96
SEC_CH = 512
CHANNELS = 2048


def draw_source_index(key, part):
    nchan = SRC // SRC_DEV
    nsect = CHANNELS // SEC_CH
    blocks = nsect * nchan
    keys = jax.random.split(key, blocks)
    picks = jax.vmap(lambda k: jax.random.permutation(k, CH_DEV)[:SRC_DEV])(keys).astype(jnp.int32)
    where_block = jnp.arange(blocks, dtype=jnp.int32) % nchan
    has_first = jnp.any(picks == 0, axis=1)
    has_last = jnp.any(picks == CH_DEV - 1, axis=1)
    set_first = (where_block == 0) & jnp.logical_not(has_first)
    set_last = (where_block == nchan - 1) & jnp.logical_not(has_last)
    column = jnp.arange(SRC_DEV, dtype=jnp.int32)[None, :] == 0
    picks = jnp.where(set_first[:, None] & column, 0, picks)
    picks = jnp.where(set_last[:, None] & column, CH_DEV - 1, picks)
    values = picks + (where_block * CH_DEV)[:, None]
    return values.reshape(nsect, SRC).astype(jnp.int32)


def block_scale(own_key, shape, cuts, smallest, top_value):
    def one(position, parts):
        heights = jax.random.uniform(jax.random.fold_in(jax.random.fold_in(own_key, 6), position), (parts,), jnp.float32, smallest / len(cuts), top_value / len(cuts))
        return jnp.repeat(jnp.exp(heights), shape[position] // parts).reshape((-1,) + (1,) * (len(shape) - position - 1))

    gain = one(*cuts[0])
    for cut in cuts[1:]:
        gain = gain * one(*cut)
    return gain


def centred(key, shape, spread, limit, shards=(), held_as=jnp.bfloat16):
    gain = block_scale(key, shape, shards, -0.22, 0.18) if shards else 1.0
    entries = jax.random.normal(key, shape, jnp.float32) * spread * gain
    return jnp.minimum(jnp.maximum(entries, -limit), limit).astype(held_as)


def setup_inputs(seed: int = 0) -> dict:
    seeds = jax.random.split(jax.random.key(seed), 5)
    return {
        "raw_traces": centred(seeds[0], (CHANNELS, NT), 1.0, 6.0, ((0, 32),)),
        "fir_taps": centred(seeds[1], (KT,), KT ** -0.5, 0.75),
        "space_taps": centred(seeds[2], (SK,), SK ** -0.5, 1.0, (), jnp.float32),
        "source_index": draw_source_index(jax.random.fold_in(seeds[4], 71), 0),
    }


def fir_matrix(taps, length):
    count = taps.shape[0]
    lead = jnp.zeros((length - 1,), taps.dtype)
    tail = jnp.zeros((length + 1 - count,), taps.dtype)
    period = jnp.concatenate([lead, taps, tail])
    flat = jnp.tile(period, length)[: length * (2 * length - 1)]
    return flat.reshape(length, 2 * length - 1)[:, length - 1:]


def space_filter(padded, space_taps, rows):
    total = jnp.zeros((rows, padded.shape[1]), jnp.float32)
    for offset in range(space_taps.shape[0]):
        total = total + space_taps[offset] * padded[offset:offset + rows].astype(jnp.float32)
    return total.astype(jnp.bfloat16)


def correlate(receivers, sources):
    rows, length = receivers.shape
    blocks = []
    for first in range(0, LAGS, 8):
        shifted = []
        for lag in range(first, first + 8):
            shifted.append(jnp.pad(receivers[:, lag:], ((0, 0), (0, lag))))
        stacked = jnp.stack(shifted, axis=1).reshape(rows * 8, length)
        block = lax.dot_general(stacked, sources, (((1,), (1,)), ((), ())), preferred_element_type=jnp.float32)
        blocks.append(block.reshape(rows, 8, sources.shape[0]))
    joined = jnp.concatenate(blocks, axis=1)
    return (joined * (1.0 / (length ** 0.5))).astype(jnp.bfloat16)


def reference(raw_traces, fir_taps, space_taps, source_index):
    length = raw_traces.shape[1]
    banded = jnp.dot(raw_traces, fir_matrix(fir_taps, length), preferred_element_type=jnp.float32).astype(jnp.bfloat16)
    half = (space_taps.shape[0] - 1) // 2
    padded = jnp.pad(banded, ((half, half), (0, 0)))
    filtered = space_filter(padded, space_taps, banded.shape[0])

    def one_section(sect):
        block = lax.dynamic_slice_in_dim(filtered, (sect * SEC_CH).astype(jnp.int32), SEC_CH, 0)
        sources = jnp.take(block, source_index[sect], axis=0)
        return correlate(block, sources)

    result = lax.map(one_section, jnp.arange(source_index.shape[0], dtype=jnp.int32))
    return result.reshape(raw_traces.shape[0], LAGS, source_index.shape[1])
```

```python
import functools

import jax
import jax.numpy as jnp
from jax import lax
from jax.experimental import pallas as pl
from jax.experimental.pallas import tpu as pltpu
from jax.sharding import PartitionSpec as P

LAGS = 64
MINOR = 8
SLOT = 8
LANES = 128
MESH = pl.DeviceIdType.MESH
F32, BF16 = jnp.float32, jnp.bfloat16


def iota(shape, dim):
    return lax.broadcasted_iota(jnp.int32, shape, dim)


def dot(a, b, contract=((1,), (0,))):
    return lax.dot_general(a, b, (contract, ((), ())), preferred_element_type=F32)


def fir_block(fir_ref, line_ref):
    taps = fir_ref.shape[1]
    line_ref[...] = jnp.zeros(line_ref.shape, F32)
    line_ref[0:1, 0:taps] = fir_ref[...].astype(F32)
    wide = jnp.broadcast_to(line_ref[0:1, 0 : 2 * LANES], (2 * LANES, 2 * LANES))
    toeplitz = pltpu.roll(wide, LANES, 1, stride=1, stride_axis=0)[:, :LANES]
    flip = (iota((LANES, LANES), 0) + iota((LANES, LANES), 1) == LANES - 1).astype(F32)
    return dot(toeplitz.astype(BF16), flip.astype(BF16)).astype(BF16)


def fir(x, block):
    rows, length = x.shape
    count = length // LANES
    parts = []
    for b in range(count):
        now = x[:, b * LANES : (b + 1) * LANES]
        before = x[:, (b - 1) * LANES : b * LANES] if b else jnp.zeros_like(now)
        parts.append(jnp.concatenate([before, now], axis=1))
    y = dot(jnp.concatenate(parts, axis=0), block).astype(BF16)
    return [y[b * rows : (b + 1) * rows] for b in reversed(range(count))]


def split3(x):
    high = x.astype(BF16)
    rest = x - high.astype(F32)
    middle = rest.astype(BF16)
    low = (rest - middle.astype(F32)).astype(BF16)
    return high, middle, low


def exchange_kernel(
    sections, chans,
    index_hbm, space_hbm, fir_hbm, raw_hbm,
    gathered_ref, far_ref, shifted_ref,
    index_ref, space_ref, fir_ref, raw_ref, line, band,
    halo, above_raw, far_rows, slope, own_ref, source_ref,
    local_sem, edge_sem, recv_sem, far_sem, slope_sem, seen, far_seen,
):
    rows, length = raw_ref.shape
    half = halo.shape[0] // 2
    sec, ch = lax.axis_index("section"), lax.axis_index("chan")
    me = sec * chans + ch
    above = sec < sections - 1
    first, final = ch == 0, ch == chans - 1
    serves = jnp.logical_and(first, sec > 0)
    served = jnp.logical_and(final, above)
    below = jnp.maximum(sec - 1, 0)
    above_id = (jnp.minimum(sec + 1, sections - 1), 0)
    prev_id = (sec, jnp.maximum(ch - 1, 0))
    next_id = (sec, jnp.minimum(ch + 1, chans - 1))

    load_raw = pltpu.make_async_copy(raw_hbm, raw_ref, local_sem.at[0])
    load_fir = pltpu.make_async_copy(fir_hbm, fir_ref, local_sem.at[1])
    load_space = pltpu.make_async_copy(space_hbm, space_ref, local_sem.at[2])
    load_index = pltpu.make_async_copy(index_hbm, index_ref, local_sem.at[3])
    load_fir.start()
    load_raw.start()
    load_space.start()
    load_index.start()

    def signal(sem, device):
        pl.semaphore_signal(sem, inc=1, device_id=device, device_id_type=MESH)

    def remote(src, dst, send, recv, device):
        return pltpu.make_async_remote_copy(
            src_ref=src, dst_ref=dst, send_sem=send, recv_sem=recv,
            device_id=device, device_id_type=MESH,
        )

    barrier = pltpu.get_barrier_semaphore()

    @pl.when(ch > 0)
    def _():
        signal(barrier, prev_id)

    for c in range(1, chans):
        @pl.when(c > ch)
        def _():
            signal(barrier, (sec, c))

    @pl.when(serves)
    def _():
        for c in range(chans - 1, 0, -1):
            signal(barrier, (below, c))

    @pl.when(jnp.logical_and(first, above))
    def _():
        signal(barrier, above_id)

    edge_send, packet_send, far_send, slope_send = (local_sem.at[i] for i in range(4))
    to_prev = remote(
        band.at[0:half], halo.at[half : 2 * half], edge_send, edge_sem, prev_id
    )
    to_next = remote(
        band.at[rows - half : rows], halo.at[0:half], edge_send, edge_sem, next_id
    )
    to_above = remote(
        raw_ref.at[rows - half : rows], above_raw, edge_send, edge_sem, above_id
    )
    edges_two = remote(halo, halo, edge_send, edge_sem, next_id)
    edges_one = remote(halo.at[0:half], halo.at[0:half], edge_send, edge_sem, next_id)

    def to_below(c):
        return remote(
            band.at[0:half], far_rows, far_send, far_sem, (below, c)
        )

    def slope_to(c):
        return remote(slope.at[chans - 1], slope.at[chans - 1], slope_send, slope_sem, (sec, c))

    def enter():
        pl.semaphore_wait(
            barrier,
            ch
            + (ch < chans - 1).astype(jnp.int32)
            + jnp.logical_and(ch > 0, above).astype(jnp.int32)
            + jnp.logical_and(first, sec > 0).astype(jnp.int32),
        )

        @pl.when(jnp.logical_and(ch > 0, above))
        def _():
            signal(far_seen, above_id)

        for c in range(chans - 2):
            @pl.when(c < ch - 1)
            def _():
                signal(seen, (sec, c))

    pl.when(final)(enter)

    load_fir.wait()
    block = fir_block(fir_ref, line)
    load_raw.wait()

    @pl.when(served)
    def _():
        to_above.start()

    for b, part in enumerate(fir(raw_ref[...], block)):
        band[:, b * LANES : (b + 1) * LANES] = part

    pl.when(jnp.logical_not(final))(enter)

    @pl.when(jnp.logical_not(final))
    def _():
        to_next.start()

    @pl.when(ch > 0)
    def _():
        to_prev.start()

    load_space.wait()
    load_index.wait()
    taps = space_ref.shape[0]

    def mixing(width, place):
        offset = place(iota((rows, width), 1)) - iota((rows, width), 0)
        mix = jnp.zeros((rows, width), F32)
        for j in range(taps):
            mix = jnp.where(offset == j, space_ref[j], mix)
        return jnp.concatenate(split3(mix), axis=1)

    mix_own = mixing(rows, lambda col: col + half)
    mix_halo = mixing(2 * half, lambda col: jnp.where(col < half, col, col + rows))
    mix_right = mixing(half, lambda col: col + half + rows)
    count = index_ref.shape[1]
    row, col = iota((2 * SLOT, rows), 0), iota((2 * SLOT, rows), 1)
    pick = jnp.zeros((2 * SLOT, rows), F32)
    for i in range(2 * SLOT):
        source = index_ref[0, i if i < count else i - (count - SLOT)] - ch * rows
        pick = jnp.where(jnp.logical_and(row == i, col == source), 1.0, pick)
    pick = pick.astype(BF16)
    source_own = dot(pick, mix_own).astype(BF16)
    source_halo = dot(pick, mix_halo).astype(BF16)

    def thrice(x):
        return jnp.concatenate([x] * 3, axis=0)

    @pl.when(served)
    def _():
        late = jnp.zeros((2 * SLOT, rows), F32)
        for i in range(count):
            source = index_ref[0, i] - ch * rows
            chosen = jnp.logical_and(row == i + 2 * SLOT - count, col == source)
            late = jnp.where(chosen, 1.0, late)
        slope[chans - 1, :, 0 : 3 * half] = dot(late.astype(BF16), mix_right).astype(BF16)
        for c in range(chans - 1):
            slope_to(c).start()

    whole = thrice(band[...])
    own_ref[...] = dot(mix_own, whole)
    source_ref[...] = dot(source_own, whole)

    @pl.when(serves)
    def _():
        pl.semaphore_wait(far_seen, chans - 1)
        for c in range(chans):
            to_below(c).start()

    @pl.when(final)
    def _():
        halo[half : 2 * half] = jnp.zeros((half, length), BF16)

    single = jnp.logical_or(final, me == 0)

    @pl.when(jnp.logical_not(single))
    def _():
        edges_two.wait_recv()

    @pl.when(single)
    def _():
        edges_one.wait_recv()

    @pl.when(serves)
    def _():
        for b, part in enumerate(fir(above_raw[...], block)):
            halo[0:half, b * LANES : (b + 1) * LANES] = part

    @pl.when(me == 0)
    def _():
        halo[0:half] = jnp.zeros((half, length), BF16)

    edges = thrice(halo[...])
    sources = source_ref[...] + dot(source_halo, edges)
    middle = length // 2
    tail = jnp.where(
        iota((SLOT, middle), 0) < SLOT // 2,
        sources[SLOT : 2 * SLOT, 0:middle], sources[SLOT : 2 * SLOT, middle:length],
    )
    gathered_ref[ch] = jnp.concatenate([sources[0:SLOT], tail], axis=1).astype(BF16)

    def packet(source, c):
        return remote(
            gathered_ref.at[source], gathered_ref.at[source],
            packet_send, recv_sem, (sec, c),
        )

    for c in range(chans - 1):
        @pl.when(c < ch)
        def _():
            packet(ch, c).start()

    @pl.when(ch < chans - 2)
    def _():
        pl.semaphore_wait(seen, chans - 2 - ch)

    for c in range(1, chans):
        @pl.when(c > ch)
        def _():
            packet(ch, c).start()

    own_ref[...] += dot(mix_halo, edges)

    @pl.when(served)
    def _():
        to_below(0).wait_recv()
        own_ref[...] += dot(mix_right, thrice(far_rows[...]))

    own_ref[...] = own_ref[...].astype(BF16).astype(F32)
    keep = iota((MINOR, length), 1) >= iota((MINOR, length), 0)
    for c in range(0, rows, 2):
        pair = []
        for r in (c, c + 1):
            wide = jnp.broadcast_to(own_ref[r : r + 1, :], (MINOR, length))
            wide = pltpu.roll(wide, 0, 1, stride=1, stride_axis=0)
            pair.append(jnp.where(keep, wide, 0.0))
        shifted_ref[c * MINOR : (c + 2) * MINOR, :] = jnp.concatenate(pair, axis=0).astype(BF16)

    @pl.when(jnp.logical_and(above, jnp.logical_not(final)))
    def _():
        to_below(0).wait_recv()
        slope_to(0).wait_recv()

    @pl.when(above)
    def _():
        far_ref[...] = dot(slope[chans - 1, :, 0 : 3 * half], thrice(far_rows[...]))

    @pl.when(jnp.logical_not(above))
    def _():
        far_ref[...] = jnp.zeros(far_ref.shape, F32)

    alone = jnp.logical_or(first, jnp.logical_and(final, jnp.logical_not(above)))

    @pl.when(jnp.logical_not(alone))
    def _():
        edges_two.wait_send()

    @pl.when(alone)
    def _():
        edges_one.wait_send()

    @pl.when(served)
    def _():
        every = slope.at[0 : chans - 1]
        remote(every, every, slope_send, slope_sem, prev_id).wait_send()

    @pl.when(serves)
    def _():
        every = shifted_ref.at[0 : chans * half]
        remote(every, every, far_send, far_sem, next_id).wait_send()

    every = gathered_ref.at[0 : chans - 1]
    packets = remote(every, every, packet_send, recv_sem, next_id)
    packets.wait_send()
    packets.wait_recv()


def correlate_kernel(per, gathered_ref, far_ref, shifted_ref, out_ref, weights, blocks, sems):
    chans, _, packet = gathered_ref.shape
    length = shifted_ref.shape[1]
    middle = packet - length
    rows, lags, total = out_ref.shape
    lanes = pl.cdiv(total, LANES) * LANES
    packets = [gathered_ref[j].astype(F32) for j in range(chans)]
    packets = jnp.concatenate(packets, axis=0).astype(BF16)
    row, col = iota((total, chans * SLOT), 0), iota((total, chans * SLOT), 1)
    inside = jnp.bitwise_and(col, SLOT - 1)
    rank = row - (lax.shift_right_logical(col, SLOT.bit_length() - 1)) * per - inside
    early = inside < SLOT // 2

    def choose(chosen):
        return jnp.where(chosen, 1.0, 0.0).astype(BF16)

    whole = choose(rank == 0)
    halves = [
        choose(jnp.logical_and(rank == SLOT, early)),
        choose(jnp.logical_and(rank == SLOT // 2, jnp.logical_not(early))),
    ]
    sources = jnp.concatenate(
        [
            dot(whole, packets[:, h * middle : (h + 1) * middle])
            + dot(halves[h], packets[:, length:packet])
            for h in range(2)
        ],
        axis=1,
    )
    edge = iota((total, LANES), 1)
    top = total - 2 * SLOT
    sources = jnp.concatenate([sources[:top], sources[top:] + far_ref[...]], axis=0)
    scale = 1.0 / length**0.5
    if lanes > total:
        for h in range(2):
            fill = jnp.zeros((weights.shape[0], lanes - total, length), BF16)
            weights[:, h * lanes + total : (h + 1) * lanes, :] = fill
    copies = []
    for k in range(lags // (2 * MINOR)):
        for h in range(2):
            shift = (2 * k + h) * MINOR
            moved = sources
            if shift:
                moved = pltpu.roll(sources, length - shift, 1)
                tail = jnp.where(edge < LANES - shift, moved[:, length - LANES :], 0.0)
                moved = jnp.concatenate([moved[:, : length - LANES], tail], axis=1)
            weights[k, h * lanes : h * lanes + total, :] = moved.astype(BF16)
        result = dot(shifted_ref[...], weights[k], ((1,), (1,))) * scale
        low = result[:, 0:total].reshape(rows, MINOR, total)
        high = result[:, lanes : lanes + total].reshape(rows, MINOR, total)
        blocks[k] = jnp.concatenate([low, high], axis=1).astype(BF16)
        copy = pltpu.make_async_copy(
            blocks.at[k], out_ref.at[:, k * 2 * MINOR : (k + 1) * 2 * MINOR, :], sems.at[k]
        )
        copy.start()
        copies.append(copy)
    for copy in copies:
        copy.wait()


def shards(sections, chans, raw_traces, fir_taps, space_taps, source_index):
    rows, length = raw_traces.shape
    half = (space_taps.shape[0] - 1) // 2
    per = source_index.shape[1]
    total = per * chans
    lanes = -(-total // LANES) * LANES
    steps = LAGS // (2 * MINOR)
    vmem, hbm = pl.BlockSpec(memory_space=pltpu.VMEM), pl.BlockSpec(memory_space=pltpu.HBM)
    gathered, far, shifted = pl.pallas_call(
        functools.partial(exchange_kernel, sections, chans),
        out_shape=(
            jax.ShapeDtypeStruct((chans, SLOT, length + length // 2), BF16),
            jax.ShapeDtypeStruct((2 * SLOT, length), F32),
            jax.ShapeDtypeStruct((rows * MINOR, length), BF16),
        ),
        in_specs=[hbm, hbm, hbm, hbm],
        out_specs=(vmem, vmem, vmem),
        scratch_shapes=[
            pltpu.SMEM(source_index.shape, jnp.int32),
            pltpu.SMEM(space_taps.shape, F32),
            pltpu.VMEM((1, fir_taps.shape[0]), BF16),
            pltpu.VMEM((rows, length), BF16),
            pltpu.VMEM((8, 2 * LANES), F32),
            pltpu.VMEM((rows, length), BF16),
            pltpu.VMEM((2 * half, length), BF16),
            pltpu.VMEM((half, length), BF16),
            pltpu.VMEM((half, length), BF16),
            pltpu.VMEM((chans, 2 * SLOT, LANES), BF16),
            pltpu.VMEM((rows, length), F32),
            pltpu.VMEM((2 * SLOT, length), F32),
            pltpu.SemaphoreType.DMA((4,)),
            pltpu.SemaphoreType.DMA,
            pltpu.SemaphoreType.DMA,
            pltpu.SemaphoreType.DMA,
            pltpu.SemaphoreType.DMA,
            pltpu.SemaphoreType.REGULAR,
            pltpu.SemaphoreType.REGULAR,
        ],
        compiler_params=pltpu.CompilerParams(
            collective_id=0, has_side_effects=True, vmem_limit_bytes=24 * 2**20
        ),
        name="exchange",
    )(
        *(
            pltpu.with_memory_space_constraint(x, pltpu.HBM)
            for x in (source_index, space_taps, fir_taps.reshape(1, -1), raw_traces)
        )
    )
    return pl.pallas_call(
        functools.partial(correlate_kernel, per),
        out_shape=jax.ShapeDtypeStruct((rows, LAGS, total), BF16),
        in_specs=[vmem, vmem, vmem],
        out_specs=pl.BlockSpec(memory_space=pl.ANY),
        scratch_shapes=[
            pltpu.VMEM((steps, 2 * lanes, length), BF16),
            pltpu.VMEM((steps, rows, 2 * MINOR, total), BF16),
            pltpu.SemaphoreType.DMA((steps,)),
        ],
        compiler_params=pltpu.CompilerParams(vmem_limit_bytes=40 * 2**20),
        name="correlate",
    )(gathered, far, shifted)


def solution(mesh):
    return jax.shard_map(
        functools.partial(shards, mesh.shape["section"], mesh.shape["chan"]),
        mesh=mesh,
        in_specs=(P(("section", "chan"), None), P(), P(), P("section", "chan")),
        out_specs=P(("section", "chan"), None, None),
        check_vma=False,
    )
```

```python
import functools

import jax
import jax.numpy as jnp
from jax import lax
from jax.experimental import pallas as pl
from jax.experimental.pallas import tpu as pltpu
from jax.sharding import PartitionSpec as P

LAGS = 64
MINOR = 8
SLOT = 8
LANES = 128
MESH = pl.DeviceIdType.MESH
F32, BF16 = jnp.float32, jnp.bfloat16


def iota(shape, dim):
    return lax.broadcasted_iota(jnp.int32, shape, dim)


def dot(a, b, contract=((1,), (0,))):
    return lax.dot_general(a, b, (contract, ((), ())), preferred_element_type=F32)


def fir_block(fir_ref, line_ref):
    taps = fir_ref.shape[1]
    line_ref[...] = jnp.zeros(line_ref.shape, F32)
    line_ref[0:1, 0:taps] = fir_ref[...].astype(F32)
    wide = jnp.broadcast_to(line_ref[0:1, 0 : 2 * LANES], (2 * LANES, 2 * LANES))
    toeplitz = pltpu.roll(wide, LANES, 1, stride=1, stride_axis=0)[:, :LANES]
    flip = (iota((LANES, LANES), 0) + iota((LANES, LANES), 1) == LANES - 1).astype(F32)
    return dot(toeplitz.astype(BF16), flip.astype(BF16)).astype(BF16)


def fir(x, block):
    rows, length = x.shape
    count = length // LANES
    parts = []
    for b in range(count):
        now = x[:, b * LANES : (b + 1) * LANES]
        before = x[:, (b - 1) * LANES : b * LANES] if b else jnp.zeros_like(now)
        parts.append(jnp.concatenate([before, now], axis=1))
    y = dot(jnp.concatenate(parts, axis=0), block).astype(BF16)
    return [y[b * rows : (b + 1) * rows] for b in reversed(range(count))]


def split3(x):
    high = x.astype(BF16)
    rest = x - high.astype(F32)
    middle = rest.astype(BF16)
    low = (rest - middle.astype(F32)).astype(BF16)
    return high, middle, low


def unpack(gathered_ref, begin, number, length):
    middle = length // 2
    upper = iota((SLOT, middle), 0) < SLOT // 2
    parts = []
    for j in range(0, number, 2):
        a, b = (gathered_ref[begin + j + i].astype(F32) for i in range(2))
        tail_a, tail_b = a[:, length:], b[:, length:]
        turn_a, turn_b = (pltpu.roll(x, SLOT // 2, 0) for x in (tail_a, tail_b))
        shared = [jnp.where(upper, tail_a, turn_b), jnp.where(upper, turn_a, tail_b)]
        parts += [a[:, :length], jnp.concatenate(shared, axis=1), b[:, :length]]
    return parts


def place(high, gathered_ref, far_ref):
    length = far_ref.shape[1]
    part = gathered_ref.shape[0] // 2
    parts = unpack(gathered_ref, jnp.where(high, part, 0), part, length)
    for i in range(2):
        parts[i - 2] += jnp.where(high, far_ref[i * SLOT : (i + 1) * SLOT], 0.0)
    scale = 1.0 / length**0.5
    even = [x * scale for x in parts]
    odd = [advance(x, MINOR) for x in even]
    count, half = len(even), LANES // 2 // SLOT
    zero = jnp.zeros((SLOT, length), F32)
    wide = [zero] * (2 * half)
    low, up = list(wide), list(wide)
    for i in range(count):
        low[i], low[half + i] = even[i], odd[i]
        up[count + i], up[(count + half + i) % (2 * half)] = even[i], odd[i]
    chosen = []
    for a, b in zip(low, up):
        chosen.append(jnp.where(high, b, a))
    return jnp.concatenate(chosen, axis=0)


def advance(x, shift):
    if not shift:
        return x
    length = x.shape[1]
    moved = pltpu.roll(x, length - shift, 1)
    edge = iota((x.shape[0], LANES), 1)
    tail = jnp.where(edge < LANES - shift, moved[:, length - LANES :], 0.0)
    return jnp.concatenate([moved[:, : length - LANES], tail], axis=1)


def correlate(per, high, gathered_ref, far_ref, shifted_ref, weights, blocks, given, finish=None):
    length = shifted_ref.shape[1]
    rows = shifted_ref.shape[0] // MINOR
    chans = gathered_ref.shape[0]
    total = per * chans
    sources = place(high, gathered_ref, far_ref)
    lane = iota((rows, 2 * MINOR, total), 2) - jnp.where(high, total // 2, 0)
    keep = jnp.logical_and(lane >= 0, lane < total // 2)
    for q in range(LAGS // (4 * MINOR)):
        for h in range(2):
            moved = advance(sources, (2 * q + h) * 2 * MINOR)
            weights[q, h * LANES : (h + 1) * LANES, :] = moved.astype(BF16)
        result = dot(shifted_ref[...], weights[q], ((1,), (1,)))
        for h in range(2):
            pair = result[:, h * LANES : (h + 1) * LANES]
            low = pair.reshape(rows, MINOR, LANES)[:, :, :total]
            top = pltpu.roll(pair, LANES // 2, 1).reshape(rows, MINOR, LANES)[:, :, :total]
            block = jnp.concatenate([low, top], axis=1).astype(BF16)
            k = 2 * q + h
            blocks[k] = block if given is None else jnp.where(keep, block, given[k])
            if finish:
                finish(k)


def exchange_kernel(
    sections, chans, per,
    index_hbm, space_hbm, fir_hbm, raw_hbm,
    gathered_ref, far_ref, shifted_ref, *rest,
):
    (
        *early, weights, index_ref, space_ref, fir_ref, raw_ref, line, band,
        halo, above_raw, far_rows, slope, own_ref, source_ref,
        local_sem, edge_sem, recv_sem, far_sem, slope_sem, seen, far_seen,
    ) = rest
    rows, length = raw_ref.shape
    half = halo.shape[0] // 2
    sec, ch = lax.axis_index("section"), lax.axis_index("chan")
    me = sec * chans + ch
    above = sec < sections - 1
    first, final = ch == 0, ch == chans - 1
    serves = jnp.logical_and(first, sec > 0)
    served = jnp.logical_and(final, above)
    below = jnp.maximum(sec - 1, 0)
    above_id = (jnp.minimum(sec + 1, sections - 1), 0)
    prev_id = (sec, jnp.maximum(ch - 1, 0))
    next_id = (sec, jnp.minimum(ch + 1, chans - 1))

    load_raw = pltpu.make_async_copy(raw_hbm, raw_ref, local_sem.at[0])
    load_fir = pltpu.make_async_copy(fir_hbm, fir_ref, local_sem.at[1])
    load_space = pltpu.make_async_copy(space_hbm, space_ref, local_sem.at[2])
    load_index = pltpu.make_async_copy(index_hbm, index_ref, local_sem.at[3])
    load_fir.start()
    load_raw.start()
    load_space.start()
    load_index.start()

    def signal(sem, device):
        pl.semaphore_signal(sem, inc=1, device_id=device, device_id_type=MESH)

    def remote(src, dst, send, recv, device):
        return pltpu.make_async_remote_copy(
            src_ref=src, dst_ref=dst, send_sem=send, recv_sem=recv,
            device_id=device, device_id_type=MESH,
        )

    barrier = pltpu.get_barrier_semaphore()

    @pl.when(ch > 0)
    def _():
        signal(barrier, prev_id)

    for c in range(1, chans):
        @pl.when(c > ch)
        def _():
            signal(barrier, (sec, c))

    @pl.when(serves)
    def _():
        for c in range(chans - 1, 0, -1):
            signal(barrier, (below, c))

    @pl.when(jnp.logical_and(first, above))
    def _():
        signal(barrier, above_id)

    edge_send, packet_send, far_send, slope_send = (local_sem.at[i] for i in range(4))
    to_prev = remote(
        band.at[0:half], halo.at[half : 2 * half], edge_send, edge_sem, prev_id
    )
    to_next = remote(
        band.at[rows - half : rows], halo.at[0:half], edge_send, edge_sem, next_id
    )
    to_above = remote(
        raw_ref.at[rows - half : rows], above_raw, edge_send, edge_sem, above_id
    )
    edges_two = remote(halo, halo, edge_send, edge_sem, next_id)
    edges_one = remote(halo.at[0:half], halo.at[0:half], edge_send, edge_sem, next_id)

    def to_below(c):
        return remote(
            band.at[0:half], far_rows, far_send, far_sem, (below, c)
        )

    def slope_to(c):
        return remote(slope.at[chans - 1], slope.at[chans - 1], slope_send, slope_sem, (sec, c))

    def enter():
        pl.semaphore_wait(
            barrier,
            ch
            + (ch < chans - 1).astype(jnp.int32)
            + jnp.logical_and(ch > 0, above).astype(jnp.int32)
            + jnp.logical_and(first, sec > 0).astype(jnp.int32),
        )

        @pl.when(jnp.logical_and(ch > 0, above))
        def _():
            signal(far_seen.at[ch], above_id)

        for c in range(chans - 2):
            @pl.when(c < ch - 1)
            def _():
                signal(seen, (sec, c))

    pl.when(final)(enter)

    load_fir.wait()
    block = fir_block(fir_ref, line)
    load_raw.wait()
    for b, part in enumerate(fir(raw_ref[...], block)):
        band[:, b * LANES : (b + 1) * LANES] = part

    pl.when(jnp.logical_not(final))(enter)

    @pl.when(jnp.logical_not(final))
    def _():
        to_next.start()

    @pl.when(ch > 0)
    def _():
        to_prev.start()

    @pl.when(served)
    def _():
        to_above.start()

    load_space.wait()
    load_index.wait()
    taps = space_ref.shape[0]

    def mixing(width, place):
        offset = place(iota((rows, width), 1)) - iota((rows, width), 0)
        mix = jnp.zeros((rows, width), F32)
        for j in range(taps):
            mix = jnp.where(offset == j, space_ref[j], mix)
        return jnp.concatenate(split3(mix), axis=1)

    mix_own = mixing(rows, lambda col: col + half)
    mix_halo = mixing(2 * half, lambda col: jnp.where(col < half, col, col + rows))
    mix_right = mixing(half, lambda col: col + half + rows)
    count = index_ref.shape[1]
    row, col = iota((2 * SLOT, rows), 0), iota((2 * SLOT, rows), 1)
    pick = jnp.zeros((2 * SLOT, rows), F32)
    odd = jnp.bitwise_and(ch, 1)
    extra = count - SLOT
    for i in range(2 * SLOT):
        which = i + extra * odd if i < SLOT else (i - SLOT) % extra + SLOT * (1 - odd)
        source = index_ref[0, which] - ch * rows
        pick = jnp.where(jnp.logical_and(row == i, col == source), 1.0, pick)
    pick = pick.astype(BF16)
    source_own = dot(pick, mix_own).astype(BF16)
    source_halo = dot(pick, mix_halo).astype(BF16)

    def thrice(x):
        return jnp.concatenate([x] * 3, axis=0)

    @pl.when(served)
    def _():
        late = jnp.zeros((2 * SLOT, rows), F32)
        for i in range(count):
            source = index_ref[0, i] - ch * rows
            chosen = jnp.logical_and(row == i + 2 * SLOT - count, col == source)
            late = jnp.where(chosen, 1.0, late)
        slope[chans - 1, :, 0 : 3 * half] = dot(late.astype(BF16), mix_right).astype(BF16)
        for c in range(chans - 1):
            slope_to(c).start()

    whole = thrice(band[...])
    own_ref[...] = dot(mix_own, whole)
    source_ref[...] = dot(source_own, whole)

    @pl.when(serves)
    def _():
        for c in range(chans):
            if c:
                pl.semaphore_wait(far_seen.at[c], 1)
            to_below(c).start()

    @pl.when(final)
    def _():
        halo[half : 2 * half] = jnp.zeros((half, length), BF16)

    single = jnp.logical_or(final, me == 0)

    @pl.when(jnp.logical_not(single))
    def _():
        edges_two.wait_recv()

    @pl.when(single)
    def _():
        edges_one.wait_recv()

    @pl.when(serves)
    def _():
        for b, part in enumerate(fir(above_raw[...], block)):
            halo[0:half, b * LANES : (b + 1) * LANES] = part

    @pl.when(me == 0)
    def _():
        halo[0:half] = jnp.zeros((half, length), BF16)

    edges = thrice(halo[...])
    sources = source_ref[...] + dot(source_halo, edges)
    middle = length // 2
    tail = jnp.where(
        iota((SLOT, middle), 0) < SLOT // 2,
        sources[SLOT : 2 * SLOT, 0:middle], sources[SLOT : 2 * SLOT, middle:length],
    )
    gathered_ref[ch] = jnp.concatenate([sources[0:SLOT], tail], axis=1).astype(BF16)

    part = chans // 2

    def packet(source, c):
        return remote(
            gathered_ref.at[source], gathered_ref.at[source],
            packet_send, recv_sem.at[((c < part) ^ (source < part)).astype(jnp.int32)], (sec, c),
        )

    for c in range(chans - 1):
        @pl.when(c < ch)
        def _():
            packet(ch, c).start()

    @pl.when(ch < chans - 2)
    def _():
        pl.semaphore_wait(seen, chans - 2 - ch)

    for c in range(1, chans):
        @pl.when(c > ch)
        def _():
            packet(ch, c).start()

    own_ref[...] += dot(mix_halo, edges)

    @pl.when(served)
    def _():
        to_below(0).wait_recv()
        own_ref[...] += dot(mix_right, thrice(far_rows[...]))

    own_ref[...] = own_ref[...].astype(BF16).astype(F32)
    keep = iota((MINOR, length), 1) >= iota((MINOR, length), 0)
    for c in range(0, rows, 2):
        pair = []
        for r in (c, c + 1):
            wide = jnp.broadcast_to(own_ref[r : r + 1, :], (MINOR, length))
            wide = pltpu.roll(wide, 0, 1, stride=1, stride_axis=0)
            pair.append(jnp.where(keep, wide, 0.0))
        shifted_ref[c * MINOR : (c + 2) * MINOR, :] = jnp.concatenate(pair, axis=0).astype(BF16)

    @pl.when(jnp.logical_and(above, jnp.logical_not(final)))
    def _():
        to_below(0).wait_recv()
        slope_to(0).wait_recv()

    @pl.when(above)
    def _():
        far_ref[...] = dot(slope[chans - 1, :, 0 : 3 * half], thrice(far_rows[...]))

    @pl.when(jnp.logical_not(above))
    def _():
        far_ref[...] = jnp.zeros(far_ref.shape, F32)

    alone = jnp.logical_or(first, jnp.logical_and(final, jnp.logical_not(above)))

    @pl.when(jnp.logical_not(alone))
    def _():
        edges_two.wait_send()

    @pl.when(alone)
    def _():
        edges_one.wait_send()

    @pl.when(served)
    def _():
        every = slope.at[0 : chans - 1]
        remote(every, every, slope_send, slope_sem, prev_id).wait_send()

    @pl.when(serves)
    def _():
        every = shifted_ref.at[0 : chans * half]
        remote(every, every, far_send, far_sem, next_id).wait_send()

    every = gathered_ref.at[0 : chans - 1]
    remote(every, every, packet_send, recv_sem.at[0], next_id).wait_send()
    near = gathered_ref.at[0 : part - 1]
    remote(near, near, packet_send, recv_sem.at[0], next_id).wait_recv()
    if early:
        correlate(per, ch >= part, gathered_ref, far_ref, shifted_ref, weights, early[0], None)
    away = gathered_ref.at[0:part]
    remote(away, away, packet_send, recv_sem.at[1], next_id).wait_recv()


def correlate_kernel(per, gathered_ref, far_ref, shifted_ref, out_ref, weights, blocks, sems):
    chans = gathered_ref.shape[0]
    length = shifted_ref.shape[1]
    rows, lags, total = out_ref.shape
    lanes = pl.cdiv(total, LANES) * LANES
    sources = jnp.concatenate(unpack(gathered_ref, 0, chans, length), axis=0)
    edge = iota((total, LANES), 1)
    top = total - 2 * SLOT
    sources = jnp.concatenate([sources[:top], sources[top:] + far_ref[...]], axis=0)
    scale = 1.0 / length**0.5
    if lanes > total:
        for h in range(2):
            fill = jnp.zeros((weights.shape[0], lanes - total, length), BF16)
            weights[:, h * lanes + total : (h + 1) * lanes, :] = fill
    copies = []
    for k in range(lags // (2 * MINOR)):
        for h in range(2):
            shift = (2 * k + h) * MINOR
            moved = sources
            if shift:
                moved = pltpu.roll(sources, length - shift, 1)
                tail = jnp.where(edge < LANES - shift, moved[:, length - LANES :], 0.0)
                moved = jnp.concatenate([moved[:, : length - LANES], tail], axis=1)
            weights[k, h * lanes : h * lanes + total, :] = moved.astype(BF16)
        result = dot(shifted_ref[...], weights[k], ((1,), (1,))) * scale
        low = result[:, 0:total].reshape(rows, MINOR, total)
        high = result[:, lanes : lanes + total].reshape(rows, MINOR, total)
        blocks[k] = jnp.concatenate([low, high], axis=1).astype(BF16)
        copy = pltpu.make_async_copy(
            blocks.at[k], out_ref.at[:, k * 2 * MINOR : (k + 1) * 2 * MINOR, :], sems.at[k]
        )
        copy.start()
        copies.append(copy)
    for copy in copies:
        copy.wait()


def finish_kernel(per, gathered_ref, far_ref, shifted_ref, early_ref, out_ref, weights, blocks, sems):
    chans = gathered_ref.shape[0]
    depth = blocks.shape[2]

    def out(k):
        return pltpu.make_async_copy(
            blocks.at[k], out_ref.at[:, k * depth : (k + 1) * depth, :], sems.at[k]
        )

    high = lax.axis_index("chan") < chans // 2
    correlate(
        per, high, gathered_ref, far_ref, shifted_ref, weights, blocks, early_ref,
        lambda k: out(k).start(),
    )
    for k in range(blocks.shape[0]):
        out(k).wait()


def shards(sections, chans, raw_traces, fir_taps, space_taps, source_index):
    rows, length = raw_traces.shape
    half = (space_taps.shape[0] - 1) // 2
    per = source_index.shape[1]
    total = per * chans
    lanes = -(-total // LANES) * LANES
    steps = LAGS // (2 * MINOR)
    vmem, hbm = pl.BlockSpec(memory_space=pltpu.VMEM), pl.BlockSpec(memory_space=pltpu.HBM)
    split = total <= LANES
    blocks = jax.ShapeDtypeStruct((steps, rows, 2 * MINOR, total), BF16)
    gathered, far, shifted, *early = pl.pallas_call(
        functools.partial(exchange_kernel, sections, chans, per),
        out_shape=(
            jax.ShapeDtypeStruct((chans, SLOT, length + length // 2), BF16),
            jax.ShapeDtypeStruct((2 * SLOT, length), F32),
            jax.ShapeDtypeStruct((rows * MINOR, length), BF16),
            *([blocks] if split else []),
        ),
        in_specs=[hbm, hbm, hbm, hbm],
        out_specs=(vmem,) * (4 if split else 3),
        scratch_shapes=[
            pltpu.VMEM((steps // 2, 2 * LANES, length), BF16),
            pltpu.SMEM(source_index.shape, jnp.int32),
            pltpu.SMEM(space_taps.shape, F32),
            pltpu.VMEM((1, fir_taps.shape[0]), BF16),
            pltpu.VMEM((rows, length), BF16),
            pltpu.VMEM((8, 2 * LANES), F32),
            pltpu.VMEM((rows, length), BF16),
            pltpu.VMEM((2 * half, length), BF16),
            pltpu.VMEM((half, length), BF16),
            pltpu.VMEM((half, length), BF16),
            pltpu.VMEM((chans, 2 * SLOT, LANES), BF16),
            pltpu.VMEM((rows, length), F32),
            pltpu.VMEM((2 * SLOT, length), F32),
            pltpu.SemaphoreType.DMA((4,)),
            pltpu.SemaphoreType.DMA,
            pltpu.SemaphoreType.DMA((2,)),
            pltpu.SemaphoreType.DMA,
            pltpu.SemaphoreType.DMA,
            pltpu.SemaphoreType.REGULAR,
            pltpu.SemaphoreType.REGULAR((chans,)),
        ],
        compiler_params=pltpu.CompilerParams(
            collective_id=0, has_side_effects=True, vmem_limit_bytes=24 * 2**20
        ),
        name="exchange",
    )(
        *(
            pltpu.with_memory_space_constraint(x, pltpu.HBM)
            for x in (source_index, space_taps, fir_taps.reshape(1, -1), raw_traces)
        )
    )
    if split:
        return pl.pallas_call(
            functools.partial(finish_kernel, per),
            out_shape=jax.ShapeDtypeStruct((rows, LAGS, total), BF16),
            in_specs=[vmem] * 4,
            out_specs=pl.BlockSpec(memory_space=pl.ANY),
            scratch_shapes=[
                pltpu.VMEM((steps // 2, 2 * LANES, length), BF16),
                pltpu.VMEM(blocks.shape, BF16),
                pltpu.SemaphoreType.DMA((steps,)),
            ],
            compiler_params=pltpu.CompilerParams(vmem_limit_bytes=40 * 2**20),
            name="finish",
        )(gathered, far, shifted, *early)
    return pl.pallas_call(
        functools.partial(correlate_kernel, per),
        out_shape=jax.ShapeDtypeStruct((rows, LAGS, total), BF16),
        in_specs=[vmem, vmem, vmem],
        out_specs=pl.BlockSpec(memory_space=pl.ANY),
        scratch_shapes=[
            pltpu.VMEM((steps, 2 * lanes, length), BF16),
            pltpu.VMEM((steps, rows, 2 * MINOR, total), BF16),
            pltpu.SemaphoreType.DMA((steps,)),
        ],
        compiler_params=pltpu.CompilerParams(vmem_limit_bytes=40 * 2**20),
        name="correlate",
    )(gathered, far, shifted)


def solution(mesh):
    return jax.shard_map(
        functools.partial(shards, mesh.shape["section"], mesh.shape["chan"]),
        mesh=mesh,
        in_specs=(P(("section", "chan"), None), P(), P(), P("section", "chan")),
        out_specs=P(("section", "chan"), None, None),
        check_vma=False,
    )
```

```python
import functools

import jax
import jax.numpy as jnp
from jax import lax
from jax.experimental import pallas as pl
from jax.experimental.pallas import tpu as pltpu
from jax.sharding import PartitionSpec as P

LAGS = 64
MINOR = 8
SLOT = 8
LANES = 128
MESH = pl.DeviceIdType.MESH
F32, BF16 = jnp.float32, jnp.bfloat16


def iota(shape, dim):
    return lax.broadcasted_iota(jnp.int32, shape, dim)


def dot(a, b, contract=((1,), (0,))):
    return lax.dot_general(a, b, (contract, ((), ())), preferred_element_type=F32)


def fir_block(fir_ref, line_ref):
    taps = fir_ref.shape[1]
    line_ref[...] = jnp.zeros(line_ref.shape, F32)
    line_ref[0:1, 0:taps] = fir_ref[...].astype(F32)
    wide = jnp.broadcast_to(line_ref[0:1, 0 : 2 * LANES], (2 * LANES, 2 * LANES))
    toeplitz = pltpu.roll(wide, LANES, 1, stride=1, stride_axis=0)[:, :LANES]
    flip = (iota((LANES, LANES), 0) + iota((LANES, LANES), 1) == LANES - 1).astype(F32)
    return dot(toeplitz.astype(BF16), flip.astype(BF16)).astype(BF16)


def fir(x, block):
    rows, length = x.shape
    count = length // LANES
    parts = []
    for b in range(count):
        now = x[:, b * LANES : (b + 1) * LANES]
        before = x[:, (b - 1) * LANES : b * LANES] if b else jnp.zeros_like(now)
        parts.append(jnp.concatenate([before, now], axis=1))
    y = dot(jnp.concatenate(parts, axis=0), block).astype(BF16)
    return [y[b * rows : (b + 1) * rows] for b in reversed(range(count))]


def split3(x):
    high = x.astype(BF16)
    rest = x - high.astype(F32)
    middle = rest.astype(BF16)
    low = (rest - middle.astype(F32)).astype(BF16)
    return high, middle, low


def unpack(gathered_ref, begin, number, length):
    middle = length // 2
    upper = iota((SLOT, middle), 0) < SLOT // 2
    parts = []
    for j in range(0, number, 2):
        a, b = (gathered_ref[begin + j + i].astype(F32) for i in range(2))
        tail_a, tail_b = a[:, length:], b[:, length:]
        turn_a, turn_b = (pltpu.roll(x, SLOT // 2, 0) for x in (tail_a, tail_b))
        shared = [jnp.where(upper, tail_a, turn_b), jnp.where(upper, turn_a, tail_b)]
        parts += [a[:, :length], jnp.concatenate(shared, axis=1), b[:, :length]]
    return parts


def place(high, gathered_ref, far_ref):
    length = far_ref.shape[1]
    part = gathered_ref.shape[0] // 2
    parts = unpack(gathered_ref, jnp.where(high, part, 0), part, length)
    for i in range(2):
        parts[i - 2] += jnp.where(high, far_ref[i * SLOT : (i + 1) * SLOT], 0.0)
    scale = 1.0 / length**0.5
    even = [x * scale for x in parts]
    odd = [advance(x, MINOR) for x in even]
    count, half = len(even), LANES // 2 // SLOT
    zero = jnp.zeros((SLOT, length), F32)
    wide = [zero] * (2 * half)
    low, up = list(wide), list(wide)
    for i in range(count):
        low[i], low[half + i] = even[i], odd[i]
        up[count + i], up[(count + half + i) % (2 * half)] = even[i], odd[i]
    chosen = []
    for a, b in zip(low, up):
        chosen.append(jnp.where(high, b, a))
    return jnp.concatenate(chosen, axis=0)


def advance(x, shift):
    if not shift:
        return x
    length = x.shape[1]
    moved = pltpu.roll(x, length - shift, 1)
    edge = iota((x.shape[0], LANES), 1)
    tail = jnp.where(edge < LANES - shift, moved[:, length - LANES :], 0.0)
    return jnp.concatenate([moved[:, : length - LANES], tail], axis=1)


def correlate(per, high, gathered_ref, far_ref, shifted_ref, weights, blocks, given, finish=None):
    length = shifted_ref.shape[1]
    rows = shifted_ref.shape[0] // MINOR
    chans = gathered_ref.shape[0]
    total = per * chans
    sources = place(high, gathered_ref, far_ref)
    lane = iota((rows, 2 * MINOR, total), 2) - jnp.where(high, total // 2, 0)
    keep = jnp.logical_and(lane >= 0, lane < total // 2)
    for q in range(LAGS // (4 * MINOR)):
        for h in range(2):
            moved = advance(sources, (2 * q + h) * 2 * MINOR)
            weights[q, h * LANES : (h + 1) * LANES, :] = moved.astype(BF16)
        result = dot(shifted_ref[...], weights[q], ((1,), (1,)))
        for h in range(2):
            pair = result[:, h * LANES : (h + 1) * LANES]
            low = pair.reshape(rows, MINOR, LANES)[:, :, :total]
            top = pltpu.roll(pair, LANES // 2, 1).reshape(rows, MINOR, LANES)[:, :, :total]
            block = jnp.concatenate([low, top], axis=1).astype(BF16)
            k = 2 * q + h
            blocks[k] = block if given is None else jnp.where(keep, block, given[k])
            if finish:
                finish(k)


def exchange_kernel(
    sections, chans, per,
    index_hbm, space_hbm, fir_hbm, raw_hbm,
    gathered_ref, far_ref, shifted_ref, *rest,
):
    (
        *early, weights, index_ref, space_ref, fir_ref, raw_ref, line, band,
        halo, above_raw, far_rows, slope, own_ref, source_ref,
        local_sem, edge_sem, recv_sem, far_sem, slope_sem, seen, far_seen,
    ) = rest
    rows, length = raw_ref.shape
    half = halo.shape[0] // 2
    sec, ch = lax.axis_index("section"), lax.axis_index("chan")
    me = sec * chans + ch
    above = sec < sections - 1
    first, final = ch == 0, ch == chans - 1
    serves = jnp.logical_and(first, sec > 0)
    served = jnp.logical_and(final, above)
    below = jnp.maximum(sec - 1, 0)
    above_id = (jnp.minimum(sec + 1, sections - 1), 0)
    prev_id = (sec, jnp.maximum(ch - 1, 0))
    next_id = (sec, jnp.minimum(ch + 1, chans - 1))

    load_raw = pltpu.make_async_copy(raw_hbm, raw_ref, local_sem.at[0])
    load_fir = pltpu.make_async_copy(fir_hbm, fir_ref, local_sem.at[1])
    load_space = pltpu.make_async_copy(space_hbm, space_ref, local_sem.at[2])
    load_index = pltpu.make_async_copy(index_hbm, index_ref, local_sem.at[3])
    load_fir.start()
    load_raw.start()
    load_space.start()
    load_index.start()

    def signal(sem, device):
        pl.semaphore_signal(sem, inc=1, device_id=device, device_id_type=MESH)

    def remote(src, dst, send, recv, device):
        return pltpu.make_async_remote_copy(
            src_ref=src, dst_ref=dst, send_sem=send, recv_sem=recv,
            device_id=device, device_id_type=MESH,
        )

    barrier = pltpu.get_barrier_semaphore()

    @pl.when(ch > 0)
    def _():
        signal(barrier, prev_id)

    for c in range(1, chans):
        @pl.when(c > ch)
        def _():
            signal(barrier, (sec, c))

    @pl.when(serves)
    def _():
        for c in range(chans - 1, 0, -1):
            signal(barrier, (below, c))

    @pl.when(jnp.logical_and(first, above))
    def _():
        signal(barrier, above_id)

    edge_send, packet_send, far_send, slope_send = (local_sem.at[i] for i in range(4))
    to_prev = remote(
        band.at[0:half], halo.at[half : 2 * half], edge_send, edge_sem, prev_id
    )
    to_next = remote(
        band.at[rows - half : rows], halo.at[0:half], edge_send, edge_sem, next_id
    )
    to_above = remote(
        raw_ref.at[rows - half : rows], above_raw, edge_send, edge_sem, above_id
    )
    edges_two = remote(halo, halo, edge_send, edge_sem, next_id)
    edges_one = remote(halo.at[0:half], halo.at[0:half], edge_send, edge_sem, next_id)

    def to_below(c):
        return remote(
            band.at[0:half], far_rows, far_send, far_sem, (below, c)
        )

    def slope_to(c):
        return remote(slope.at[chans - 1], slope.at[chans - 1], slope_send, slope_sem, (sec, c))

    def enter():
        pl.semaphore_wait(
            barrier,
            ch
            + (ch < chans - 1).astype(jnp.int32)
            + jnp.logical_and(ch > 0, above).astype(jnp.int32)
            + jnp.logical_and(first, sec > 0).astype(jnp.int32),
        )

        @pl.when(jnp.logical_and(ch > 0, above))
        def _():
            signal(far_seen.at[ch], above_id)

        for c in range(chans - 2):
            @pl.when(c < ch - 1)
            def _():
                signal(seen, (sec, c))

    pl.when(final)(enter)

    load_fir.wait()
    block = fir_block(fir_ref, line)
    load_raw.wait()
    for b, part in enumerate(fir(raw_ref[...], block)):
        band[:, b * LANES : (b + 1) * LANES] = part

    pl.when(jnp.logical_not(final))(enter)

    @pl.when(jnp.logical_not(final))
    def _():
        to_next.start()

    @pl.when(ch > 0)
    def _():
        to_prev.start()

    @pl.when(served)
    def _():
        to_above.start()

    load_space.wait()
    load_index.wait()
    taps = space_ref.shape[0]

    def mixing(width, place):
        offset = place(iota((rows, width), 1)) - iota((rows, width), 0)
        mix = jnp.zeros((rows, width), F32)
        for j in range(taps):
            mix = jnp.where(offset == j, space_ref[j], mix)
        return jnp.concatenate(split3(mix), axis=1)

    mix_own = mixing(rows, lambda col: col + half)
    mix_halo = mixing(2 * half, lambda col: jnp.where(col < half, col, col + rows))
    mix_right = mixing(half, lambda col: col + half + rows)
    count = index_ref.shape[1]
    row, col = iota((2 * SLOT, rows), 0), iota((2 * SLOT, rows), 1)
    pick = jnp.zeros((2 * SLOT, rows), F32)
    odd = jnp.bitwise_and(ch, 1)
    extra = count - SLOT
    for i in range(2 * SLOT):
        which = i + extra * odd if i < SLOT else (i - SLOT) % extra + SLOT * (1 - odd)
        source = index_ref[0, which] - ch * rows
        pick = jnp.where(jnp.logical_and(row == i, col == source), 1.0, pick)
    pick = pick.astype(BF16)
    source_own = dot(pick, mix_own).astype(BF16)
    source_halo = dot(pick, mix_halo).astype(BF16)

    def thrice(x):
        return jnp.concatenate([x] * 3, axis=0)

    @pl.when(served)
    def _():
        late = jnp.zeros((2 * SLOT, rows), F32)
        for i in range(count):
            source = index_ref[0, i] - ch * rows
            chosen = jnp.logical_and(row == i + 2 * SLOT - count, col == source)
            late = jnp.where(chosen, 1.0, late)
        slope[chans - 1, :, 0 : 3 * half] = dot(late.astype(BF16), mix_right).astype(BF16)

    whole = thrice(band[...])
    own_ref[...] = dot(mix_own, whole)
    source_ref[...] = dot(source_own, whole)

    @pl.when(served)
    def _():
        for c in range(chans - 1):
            slope_to(c).start()

    @pl.when(serves)
    def _():
        for c in range(chans):
            if c:
                pl.semaphore_wait(far_seen.at[c], 1)
            to_below(c).start()

    @pl.when(final)
    def _():
        halo[half : 2 * half] = jnp.zeros((half, length), BF16)

    single = jnp.logical_or(final, me == 0)

    @pl.when(jnp.logical_not(single))
    def _():
        edges_two.wait_recv()

    @pl.when(single)
    def _():
        edges_one.wait_recv()

    @pl.when(serves)
    def _():
        for b, part in enumerate(fir(above_raw[...], block)):
            halo[0:half, b * LANES : (b + 1) * LANES] = part

    @pl.when(me == 0)
    def _():
        halo[0:half] = jnp.zeros((half, length), BF16)

    edges = thrice(halo[...])
    sources = source_ref[...] + dot(source_halo, edges)
    middle = length // 2
    tail = jnp.where(
        iota((SLOT, middle), 0) < SLOT // 2,
        sources[SLOT : 2 * SLOT, 0:middle], sources[SLOT : 2 * SLOT, middle:length],
    )
    gathered_ref[ch] = jnp.concatenate([sources[0:SLOT], tail], axis=1).astype(BF16)

    part = chans // 2

    def packet(source, c):
        return remote(
            gathered_ref.at[source], gathered_ref.at[source],
            packet_send, recv_sem.at[((c < part) ^ (source < part)).astype(jnp.int32)], (sec, c),
        )

    for c in range(2):
        @pl.when(c < ch)
        def _():
            packet(ch, c).start()

    @pl.when(ch < chans - 2)
    def _():
        pl.semaphore_wait(seen, chans - 2 - ch)

    for c in range(1, chans):
        @pl.when(c > ch)
        def _():
            packet(ch, c).start()

    for c in range(chans - 2, 1, -1):
        @pl.when(c < ch)
        def _():
            packet(ch, c).start()

    own_ref[...] += dot(mix_halo, edges)

    @pl.when(served)
    def _():
        to_below(0).wait_recv()
        own_ref[...] += dot(mix_right, thrice(far_rows[...]))

    own_ref[...] = own_ref[...].astype(BF16).astype(F32)
    keep = iota((MINOR, length), 1) >= iota((MINOR, length), 0)
    for c in range(0, rows, 2):
        pair = []
        for r in (c, c + 1):
            wide = jnp.broadcast_to(own_ref[r : r + 1, :], (MINOR, length))
            wide = pltpu.roll(wide, 0, 1, stride=1, stride_axis=0)
            pair.append(jnp.where(keep, wide, 0.0))
        shifted_ref[c * MINOR : (c + 2) * MINOR, :] = jnp.concatenate(pair, axis=0).astype(BF16)

    @pl.when(jnp.logical_and(above, jnp.logical_not(final)))
    def _():
        to_below(0).wait_recv()
        slope_to(0).wait_recv()

    @pl.when(above)
    def _():
        far_ref[...] = dot(slope[chans - 1, :, 0 : 3 * half], thrice(far_rows[...]))

    @pl.when(jnp.logical_not(above))
    def _():
        far_ref[...] = jnp.zeros(far_ref.shape, F32)

    near = gathered_ref.at[0 : part - 1]
    remote(near, near, packet_send, recv_sem.at[0], next_id).wait_recv()
    if early:
        correlate(per, ch >= part, gathered_ref, far_ref, shifted_ref, weights, early[0], None)
    alone = jnp.logical_or(first, jnp.logical_and(final, jnp.logical_not(above)))

    @pl.when(jnp.logical_not(alone))
    def _():
        edges_two.wait_send()

    @pl.when(alone)
    def _():
        edges_one.wait_send()

    @pl.when(served)
    def _():
        every = slope.at[0 : chans - 1]
        remote(every, every, slope_send, slope_sem, prev_id).wait_send()

    @pl.when(serves)
    def _():
        every = shifted_ref.at[0 : chans * half]
        remote(every, every, far_send, far_sem, next_id).wait_send()

    every = gathered_ref.at[0 : chans - 1]
    remote(every, every, packet_send, recv_sem.at[0], next_id).wait_send()
    away = gathered_ref.at[0:part]
    remote(away, away, packet_send, recv_sem.at[1], next_id).wait_recv()


def correlate_kernel(per, gathered_ref, far_ref, shifted_ref, out_ref, weights, blocks, sems):
    chans = gathered_ref.shape[0]
    length = shifted_ref.shape[1]
    rows, lags, total = out_ref.shape
    lanes = pl.cdiv(total, LANES) * LANES
    sources = jnp.concatenate(unpack(gathered_ref, 0, chans, length), axis=0)
    edge = iota((total, LANES), 1)
    top = total - 2 * SLOT
    sources = jnp.concatenate([sources[:top], sources[top:] + far_ref[...]], axis=0)
    scale = 1.0 / length**0.5
    if lanes > total:
        for h in range(2):
            fill = jnp.zeros((weights.shape[0], lanes - total, length), BF16)
            weights[:, h * lanes + total : (h + 1) * lanes, :] = fill
    copies = []
    for k in range(lags // (2 * MINOR)):
        for h in range(2):
            shift = (2 * k + h) * MINOR
            moved = sources
            if shift:
                moved = pltpu.roll(sources, length - shift, 1)
                tail = jnp.where(edge < LANES - shift, moved[:, length - LANES :], 0.0)
                moved = jnp.concatenate([moved[:, : length - LANES], tail], axis=1)
            weights[k, h * lanes : h * lanes + total, :] = moved.astype(BF16)
        result = dot(shifted_ref[...], weights[k], ((1,), (1,))) * scale
        low = result[:, 0:total].reshape(rows, MINOR, total)
        high = result[:, lanes : lanes + total].reshape(rows, MINOR, total)
        blocks[k] = jnp.concatenate([low, high], axis=1).astype(BF16)
        copy = pltpu.make_async_copy(
            blocks.at[k], out_ref.at[:, k * 2 * MINOR : (k + 1) * 2 * MINOR, :], sems.at[k]
        )
        copy.start()
        copies.append(copy)
    for copy in copies:
        copy.wait()


def finish_kernel(per, gathered_ref, far_ref, shifted_ref, early_ref, out_ref, weights, blocks, sems):
    chans = gathered_ref.shape[0]
    depth = blocks.shape[2]

    def out(k):
        return pltpu.make_async_copy(
            blocks.at[k], out_ref.at[:, k * depth : (k + 1) * depth, :], sems.at[k]
        )

    high = lax.axis_index("chan") < chans // 2
    correlate(
        per, high, gathered_ref, far_ref, shifted_ref, weights, blocks, early_ref,
        lambda k: out(k).start(),
    )
    for k in range(blocks.shape[0]):
        out(k).wait()


def shards(sections, chans, raw_traces, fir_taps, space_taps, source_index):
    rows, length = raw_traces.shape
    half = (space_taps.shape[0] - 1) // 2
    per = source_index.shape[1]
    total = per * chans
    lanes = -(-total // LANES) * LANES
    steps = LAGS // (2 * MINOR)
    vmem, hbm = pl.BlockSpec(memory_space=pltpu.VMEM), pl.BlockSpec(memory_space=pltpu.HBM)
    split = total <= LANES
    blocks = jax.ShapeDtypeStruct((steps, rows, 2 * MINOR, total), BF16)
    gathered, far, shifted, *early = pl.pallas_call(
        functools.partial(exchange_kernel, sections, chans, per),
        out_shape=(
            jax.ShapeDtypeStruct((chans, SLOT, length + length // 2), BF16),
            jax.ShapeDtypeStruct((2 * SLOT, length), F32),
            jax.ShapeDtypeStruct((rows * MINOR, length), BF16),
            *([blocks] if split else []),
        ),
        in_specs=[hbm, hbm, hbm, hbm],
        out_specs=(vmem,) * (4 if split else 3),
        scratch_shapes=[
            pltpu.VMEM((steps // 2, 2 * LANES, length), BF16),
            pltpu.SMEM(source_index.shape, jnp.int32),
            pltpu.SMEM(space_taps.shape, F32),
            pltpu.VMEM((1, fir_taps.shape[0]), BF16),
            pltpu.VMEM((rows, length), BF16),
            pltpu.VMEM((8, 2 * LANES), F32),
            pltpu.VMEM((rows, length), BF16),
            pltpu.VMEM((2 * half, length), BF16),
            pltpu.VMEM((half, length), BF16),
            pltpu.VMEM((half, length), BF16),
            pltpu.VMEM((chans, 2 * SLOT, LANES), BF16),
            pltpu.VMEM((rows, length), F32),
            pltpu.VMEM((2 * SLOT, length), F32),
            pltpu.SemaphoreType.DMA((4,)),
            pltpu.SemaphoreType.DMA,
            pltpu.SemaphoreType.DMA((2,)),
            pltpu.SemaphoreType.DMA,
            pltpu.SemaphoreType.DMA,
            pltpu.SemaphoreType.REGULAR,
            pltpu.SemaphoreType.REGULAR((chans,)),
        ],
        compiler_params=pltpu.CompilerParams(
            collective_id=0, has_side_effects=True, vmem_limit_bytes=24 * 2**20
        ),
        name="exchange",
    )(
        *(
            pltpu.with_memory_space_constraint(x, pltpu.HBM)
            for x in (source_index, space_taps, fir_taps.reshape(1, -1), raw_traces)
        )
    )
    if split:
        return pl.pallas_call(
            functools.partial(finish_kernel, per),
            out_shape=jax.ShapeDtypeStruct((rows, LAGS, total), BF16),
            in_specs=[vmem] * 4,
            out_specs=pl.BlockSpec(memory_space=pl.ANY),
            scratch_shapes=[
                pltpu.VMEM((steps // 2, 2 * LANES, length), BF16),
                pltpu.VMEM(blocks.shape, BF16),
                pltpu.SemaphoreType.DMA((steps,)),
            ],
            compiler_params=pltpu.CompilerParams(vmem_limit_bytes=40 * 2**20),
            name="finish",
        )(gathered, far, shifted, *early)
    return pl.pallas_call(
        functools.partial(correlate_kernel, per),
        out_shape=jax.ShapeDtypeStruct((rows, LAGS, total), BF16),
        in_specs=[vmem, vmem, vmem],
        out_specs=pl.BlockSpec(memory_space=pl.ANY),
        scratch_shapes=[
            pltpu.VMEM((steps, 2 * lanes, length), BF16),
            pltpu.VMEM((steps, rows, 2 * MINOR, total), BF16),
            pltpu.SemaphoreType.DMA((steps,)),
        ],
        compiler_params=pltpu.CompilerParams(vmem_limit_bytes=40 * 2**20),
        name="correlate",
    )(gathered, far, shifted)


def solution(mesh):
    return jax.shard_map(
        functools.partial(shards, mesh.shape["section"], mesh.shape["chan"]),
        mesh=mesh,
        in_specs=(P(("section", "chan"), None), P(), P(), P("section", "chan")),
        out_specs=P(("section", "chan"), None, None),
        check_vma=False,
    )
```

```python
import functools

import jax
import jax.numpy as jnp
from jax import lax
from jax.experimental import pallas as pl
from jax.experimental.pallas import tpu as pltpu
from jax.sharding import PartitionSpec as P

LAGS = 64
MINOR = 16
SLOT = 8
LANES = 128
MESH = pl.DeviceIdType.MESH
F32, BF16 = jnp.float32, jnp.bfloat16


def iota(shape, dim):
    return lax.broadcasted_iota(jnp.int32, shape, dim)


def dot(a, b, contract=((1,), (0,))):
    return lax.dot_general(a, b, (contract, ((), ())), preferred_element_type=F32)


def fir_block(fir_ref, line_ref):
    taps = fir_ref.shape[1]
    line_ref[...] = jnp.zeros(line_ref.shape, F32)
    line_ref[0:1, 0:taps] = fir_ref[...].astype(F32)
    wide = jnp.broadcast_to(line_ref[0:1, 0 : 2 * LANES], (2 * LANES, 2 * LANES))
    toeplitz = pltpu.roll(wide, LANES, 1, stride=1, stride_axis=0)[:, :LANES]
    flip = (iota((LANES, LANES), 0) + iota((LANES, LANES), 1) == LANES - 1).astype(F32)
    return dot(toeplitz.astype(BF16), flip.astype(BF16)).astype(BF16)


def fir(x, block):
    rows, length = x.shape
    count = length // LANES
    parts = []
    for b in range(count):
        now = x[:, b * LANES : (b + 1) * LANES]
        before = x[:, (b - 1) * LANES : b * LANES] if b else jnp.zeros_like(now)
        parts.append(jnp.concatenate([before, now], axis=1))
    y = dot(jnp.concatenate(parts, axis=0), block).astype(BF16)
    return [y[b * rows : (b + 1) * rows] for b in reversed(range(count))]


def split3(x):
    high = x.astype(BF16)
    rest = x - high.astype(F32)
    middle = rest.astype(BF16)
    low = (rest - middle.astype(F32)).astype(BF16)
    return high, middle, low


def unpack(gathered_ref, begin, number, length):
    middle = length // 2
    upper = iota((SLOT, middle), 0) < SLOT // 2
    parts = []
    for j in range(0, number, 2):
        a, b = (gathered_ref[begin + j + i].astype(F32) for i in range(2))
        tail_a, tail_b = a[:, length:], b[:, length:]
        turn_a, turn_b = (pltpu.roll(x, SLOT // 2, 0) for x in (tail_a, tail_b))
        shared = [jnp.where(upper, tail_a, turn_b), jnp.where(upper, turn_a, tail_b)]
        parts += [a[:, :length], jnp.concatenate(shared, axis=1), b[:, :length]]
    return parts


def place(high, gathered_ref, far_ref):
    length = far_ref.shape[1]
    part = gathered_ref.shape[0] // 2
    parts = unpack(gathered_ref, jnp.where(high, part, 0), part, length)
    for i in range(2):
        parts[i - 2] += jnp.where(high, far_ref[i * SLOT : (i + 1) * SLOT], 0.0)
    scale = 1.0 / length**0.5
    even = [x * scale for x in parts]
    odd = [advance(x, MINOR) for x in even]
    count, half = len(even), LANES // 2 // SLOT
    zero = jnp.zeros((SLOT, length), F32)
    wide = [zero] * (2 * half)
    low, up = list(wide), list(wide)
    for i in range(count):
        low[i], low[half + i] = even[i], odd[i]
        up[count + i], up[(count + half + i) % (2 * half)] = even[i], odd[i]
    chosen = []
    for a, b in zip(low, up):
        chosen.append(jnp.where(high, b, a))
    return jnp.concatenate(chosen, axis=0)


def advance(x, shift):
    if not shift:
        return x
    length = x.shape[1]
    moved = pltpu.roll(x, length - shift, 1)
    edge = iota((x.shape[0], LANES), 1)
    tail = jnp.where(edge < LANES - shift, moved[:, length - LANES :], 0.0)
    return jnp.concatenate([moved[:, : length - LANES], tail], axis=1)


def correlate(per, high, gathered_ref, far_ref, shifted_ref, weights, blocks, given, finish=None):
    length = shifted_ref.shape[1]
    rows = shifted_ref.shape[0] // MINOR
    chans = gathered_ref.shape[0]
    total = per * chans
    sources = place(high, gathered_ref, far_ref)
    lane = iota((rows, MINOR, total), 2) - jnp.where(high, total // 2, 0)
    keep = jnp.logical_and(lane >= 0, lane < total // 2)
    for h in range(2):
        moved = advance(sources, h * 2 * MINOR)
        weights[h * LANES : (h + 1) * LANES, :] = moved.astype(BF16)
    result = dot(shifted_ref[...], weights[...], ((1,), (1,)))
    for h in range(2):
        pair = result[:, h * LANES : (h + 1) * LANES]
        for i in range(2):
            turned = pltpu.roll(pair, LANES // 2, 1) if i else pair
            block = turned.reshape(rows, MINOR, LANES)[:, :, :total].astype(BF16)
            k = 2 * h + i
            blocks[k] = block if given is None else jnp.where(keep, block, given[k])
            if finish:
                finish(k)


def exchange_kernel(
    sections, chans, per,
    index_hbm, space_hbm, fir_hbm, raw_hbm,
    gathered_ref, far_ref, shifted_ref, *rest,
):
    (
        *early, weights, index_ref, space_ref, fir_ref, raw_ref, line, band,
        halo, above_raw, far_rows, slope, own_ref, source_ref,
        local_sem, edge_sem, recv_sem, far_sem, slope_sem, seen, far_seen,
    ) = rest
    rows, length = raw_ref.shape
    half = halo.shape[0] // 2
    sec, ch = lax.axis_index("section"), lax.axis_index("chan")
    me = sec * chans + ch
    above = sec < sections - 1
    first, final = ch == 0, ch == chans - 1
    serves = jnp.logical_and(first, sec > 0)
    served = jnp.logical_and(final, above)
    below = jnp.maximum(sec - 1, 0)
    above_id = (jnp.minimum(sec + 1, sections - 1), 0)
    prev_id = (sec, jnp.maximum(ch - 1, 0))
    next_id = (sec, jnp.minimum(ch + 1, chans - 1))

    load_raw = pltpu.make_async_copy(raw_hbm, raw_ref, local_sem.at[0])
    load_fir = pltpu.make_async_copy(fir_hbm, fir_ref, local_sem.at[1])
    load_space = pltpu.make_async_copy(space_hbm, space_ref, local_sem.at[2])
    load_index = pltpu.make_async_copy(index_hbm, index_ref, local_sem.at[3])
    load_fir.start()
    load_raw.start()
    load_space.start()
    load_index.start()

    def signal(sem, device):
        pl.semaphore_signal(sem, inc=1, device_id=device, device_id_type=MESH)

    def remote(src, dst, send, recv, device):
        return pltpu.make_async_remote_copy(
            src_ref=src, dst_ref=dst, send_sem=send, recv_sem=recv,
            device_id=device, device_id_type=MESH,
        )

    barrier = pltpu.get_barrier_semaphore()

    @pl.when(ch > 0)
    def _():
        signal(barrier, prev_id)

    for c in range(1, chans):
        @pl.when(c > ch)
        def _():
            signal(barrier, (sec, c))

    @pl.when(serves)
    def _():
        for c in range(chans - 1, 0, -1):
            signal(barrier, (below, c))

    @pl.when(jnp.logical_and(first, above))
    def _():
        signal(barrier, above_id)

    edge_send, packet_send, far_send, slope_send = (local_sem.at[i] for i in range(4))
    to_prev = remote(
        band.at[0:half], halo.at[half : 2 * half], edge_send, edge_sem, prev_id
    )
    to_next = remote(
        band.at[rows - half : rows], halo.at[0:half], edge_send, edge_sem, next_id
    )
    to_above = remote(
        raw_ref.at[rows - half : rows], above_raw, edge_send, edge_sem, above_id
    )
    edges_two = remote(halo, halo, edge_send, edge_sem, next_id)
    edges_one = remote(halo.at[0:half], halo.at[0:half], edge_send, edge_sem, next_id)

    def to_below(c):
        return remote(
            band.at[0:half], far_rows, far_send, far_sem, (below, c)
        )

    def slope_to(c):
        return remote(slope.at[chans - 1], slope.at[chans - 1], slope_send, slope_sem, (sec, c))

    def enter():
        pl.semaphore_wait(
            barrier,
            ch
            + (ch < chans - 1).astype(jnp.int32)
            + jnp.logical_and(ch > 0, above).astype(jnp.int32)
            + jnp.logical_and(first, sec > 0).astype(jnp.int32),
        )

        @pl.when(jnp.logical_and(ch > 0, above))
        def _():
            signal(far_seen.at[ch], above_id)

        for c in range(chans - 2):
            @pl.when(c < ch - 1)
            def _():
                signal(seen, (sec, c))

    pl.when(final)(enter)

    load_fir.wait()
    block = fir_block(fir_ref, line)
    load_raw.wait()
    for b, part in enumerate(fir(raw_ref[...], block)):
        band[:, b * LANES : (b + 1) * LANES] = part

    pl.when(jnp.logical_not(final))(enter)

    @pl.when(jnp.logical_not(final))
    def _():
        to_next.start()

    @pl.when(ch > 0)
    def _():
        to_prev.start()

    @pl.when(served)
    def _():
        to_above.start()

    load_space.wait()
    load_index.wait()
    taps = space_ref.shape[0]

    def mixing(width, place):
        offset = place(iota((rows, width), 1)) - iota((rows, width), 0)
        mix = jnp.zeros((rows, width), F32)
        for j in range(taps):
            mix = jnp.where(offset == j, space_ref[j], mix)
        return jnp.concatenate(split3(mix), axis=1)

    mix_own = mixing(rows, lambda col: col + half)
    mix_halo = mixing(2 * half, lambda col: jnp.where(col < half, col, col + rows))
    mix_right = mixing(half, lambda col: col + half + rows)
    count = index_ref.shape[1]
    row, col = iota((2 * SLOT, rows), 0), iota((2 * SLOT, rows), 1)
    pick = jnp.zeros((2 * SLOT, rows), F32)
    odd = jnp.bitwise_and(ch, 1)
    extra = count - SLOT
    for i in range(2 * SLOT):
        which = i + extra * odd if i < SLOT else (i - SLOT) % extra + SLOT * (1 - odd)
        source = index_ref[0, which] - ch * rows
        pick = jnp.where(jnp.logical_and(row == i, col == source), 1.0, pick)
    pick = pick.astype(BF16)
    source_own = dot(pick, mix_own).astype(BF16)
    source_halo = dot(pick, mix_halo).astype(BF16)

    def thrice(x):
        return jnp.concatenate([x] * 3, axis=0)

    @pl.when(served)
    def _():
        late = jnp.zeros((2 * SLOT, rows), F32)
        for i in range(count):
            source = index_ref[0, i] - ch * rows
            chosen = jnp.logical_and(row == i + 2 * SLOT - count, col == source)
            late = jnp.where(chosen, 1.0, late)
        slope[chans - 1, :, 0 : 3 * half] = dot(late.astype(BF16), mix_right).astype(BF16)

    whole = thrice(band[...])
    own_ref[...] = dot(mix_own, whole)
    source_ref[...] = dot(source_own, whole)

    @pl.when(served)
    def _():
        for c in range(chans - 1):
            slope_to(c).start()

    @pl.when(serves)
    def _():
        for c in range(chans):
            if c:
                pl.semaphore_wait(far_seen.at[c], 1)
            to_below(c).start()

    @pl.when(final)
    def _():
        halo[half : 2 * half] = jnp.zeros((half, length), BF16)

    single = jnp.logical_or(final, me == 0)

    @pl.when(jnp.logical_not(single))
    def _():
        edges_two.wait_recv()

    @pl.when(single)
    def _():
        edges_one.wait_recv()

    @pl.when(serves)
    def _():
        for b, part in enumerate(fir(above_raw[...], block)):
            halo[0:half, b * LANES : (b + 1) * LANES] = part

    @pl.when(me == 0)
    def _():
        halo[0:half] = jnp.zeros((half, length), BF16)

    edges = thrice(halo[...])
    sources = source_ref[...] + dot(source_halo, edges)
    middle = length // 2
    tail = jnp.where(
        iota((SLOT, middle), 0) < SLOT // 2,
        sources[SLOT : 2 * SLOT, 0:middle], sources[SLOT : 2 * SLOT, middle:length],
    )
    gathered_ref[ch] = jnp.concatenate([sources[0:SLOT], tail], axis=1).astype(BF16)

    part = chans // 2

    def packet(source, c):
        return remote(
            gathered_ref.at[source], gathered_ref.at[source],
            packet_send, recv_sem.at[((c < part) ^ (source < part)).astype(jnp.int32)], (sec, c),
        )

    for c in range(2):
        @pl.when(c < ch)
        def _():
            packet(ch, c).start()

    @pl.when(ch < chans - 2)
    def _():
        pl.semaphore_wait(seen, chans - 2 - ch)

    for c in range(1, chans):
        @pl.when(c > ch)
        def _():
            packet(ch, c).start()

    for c in range(chans - 2, 1, -1):
        @pl.when(c < ch)
        def _():
            packet(ch, c).start()

    own_ref[...] += dot(mix_halo, edges)

    @pl.when(served)
    def _():
        to_below(0).wait_recv()
        own_ref[...] += dot(mix_right, thrice(far_rows[...]))

    own_ref[...] = own_ref[...].astype(BF16).astype(F32)
    keep = iota((MINOR, length), 1) >= iota((MINOR, length), 0)
    for c in range(rows):
        wide = jnp.broadcast_to(own_ref[c : c + 1, :], (MINOR, length))
        wide = pltpu.roll(wide, 0, 1, stride=1, stride_axis=0)
        shifted_ref[c * MINOR : (c + 1) * MINOR, :] = jnp.where(keep, wide, 0.0).astype(BF16)

    @pl.when(jnp.logical_and(above, jnp.logical_not(final)))
    def _():
        to_below(0).wait_recv()
        slope_to(0).wait_recv()

    @pl.when(above)
    def _():
        far_ref[...] = dot(slope[chans - 1, :, 0 : 3 * half], thrice(far_rows[...]))

    @pl.when(jnp.logical_not(above))
    def _():
        far_ref[...] = jnp.zeros(far_ref.shape, F32)

    near = gathered_ref.at[0 : part - 1]
    remote(near, near, packet_send, recv_sem.at[0], next_id).wait_recv()
    if early:
        correlate(per, ch >= part, gathered_ref, far_ref, shifted_ref, weights, early[0], None)
    alone = jnp.logical_or(first, jnp.logical_and(final, jnp.logical_not(above)))

    @pl.when(jnp.logical_not(alone))
    def _():
        edges_two.wait_send()

    @pl.when(alone)
    def _():
        edges_one.wait_send()

    @pl.when(served)
    def _():
        every = slope.at[0 : chans - 1]
        remote(every, every, slope_send, slope_sem, prev_id).wait_send()

    @pl.when(serves)
    def _():
        every = shifted_ref.at[0 : chans * half]
        remote(every, every, far_send, far_sem, next_id).wait_send()

    every = gathered_ref.at[0 : chans - 1]
    remote(every, every, packet_send, recv_sem.at[0], next_id).wait_send()
    away = gathered_ref.at[0:part]
    remote(away, away, packet_send, recv_sem.at[1], next_id).wait_recv()


def correlate_kernel(per, gathered_ref, far_ref, shifted_ref, out_ref, weights, blocks, sems):
    chans = gathered_ref.shape[0]
    length = shifted_ref.shape[1]
    rows, lags, total = out_ref.shape
    lanes = pl.cdiv(total, LANES) * LANES
    sources = jnp.concatenate(unpack(gathered_ref, 0, chans, length), axis=0)
    edge = iota((total, LANES), 1)
    top = total - 2 * SLOT
    sources = jnp.concatenate([sources[:top], sources[top:] + far_ref[...]], axis=0)
    scale = 1.0 / length**0.5
    if lanes > total:
        for h in range(2):
            fill = jnp.zeros((weights.shape[0], lanes - total, length), BF16)
            weights[:, h * lanes + total : (h + 1) * lanes, :] = fill
    copies = []
    for k in range(lags // (2 * MINOR)):
        for h in range(2):
            shift = (2 * k + h) * MINOR
            moved = sources
            if shift:
                moved = pltpu.roll(sources, length - shift, 1)
                tail = jnp.where(edge < LANES - shift, moved[:, length - LANES :], 0.0)
                moved = jnp.concatenate([moved[:, : length - LANES], tail], axis=1)
            weights[k, h * lanes : h * lanes + total, :] = moved.astype(BF16)
        result = dot(shifted_ref[...], weights[k], ((1,), (1,))) * scale
        low = result[:, 0:total].reshape(rows, MINOR, total)
        high = result[:, lanes : lanes + total].reshape(rows, MINOR, total)
        blocks[k] = jnp.concatenate([low, high], axis=1).astype(BF16)
        copy = pltpu.make_async_copy(
            blocks.at[k], out_ref.at[:, k * 2 * MINOR : (k + 1) * 2 * MINOR, :], sems.at[k]
        )
        copy.start()
        copies.append(copy)
    for copy in copies:
        copy.wait()


def finish_kernel(per, gathered_ref, far_ref, shifted_ref, early_ref, out_ref, weights, blocks, sems):
    chans = gathered_ref.shape[0]
    depth = blocks.shape[2]

    def out(k):
        return pltpu.make_async_copy(
            blocks.at[k], out_ref.at[:, k * depth : (k + 1) * depth, :], sems.at[k]
        )

    high = lax.axis_index("chan") < chans // 2
    correlate(
        per, high, gathered_ref, far_ref, shifted_ref, weights, blocks, early_ref,
        lambda k: out(k).start(),
    )
    for k in range(blocks.shape[0]):
        out(k).wait()


def shards(sections, chans, raw_traces, fir_taps, space_taps, source_index):
    rows, length = raw_traces.shape
    half = (space_taps.shape[0] - 1) // 2
    per = source_index.shape[1]
    total = per * chans
    lanes = -(-total // LANES) * LANES
    steps = LAGS // (2 * MINOR)
    vmem, hbm = pl.BlockSpec(memory_space=pltpu.VMEM), pl.BlockSpec(memory_space=pltpu.HBM)
    split = total <= LANES
    blocks = jax.ShapeDtypeStruct((LAGS // MINOR, rows, MINOR, total), BF16)
    gathered, far, shifted, *early = pl.pallas_call(
        functools.partial(exchange_kernel, sections, chans, per),
        out_shape=(
            jax.ShapeDtypeStruct((chans, SLOT, length + length // 2), BF16),
            jax.ShapeDtypeStruct((2 * SLOT, length), F32),
            jax.ShapeDtypeStruct((rows * MINOR, length), BF16),
            *([blocks] if split else []),
        ),
        in_specs=[hbm, hbm, hbm, hbm],
        out_specs=(vmem,) * (4 if split else 3),
        scratch_shapes=[
            pltpu.VMEM((2 * LANES, length), BF16),
            pltpu.SMEM(source_index.shape, jnp.int32),
            pltpu.SMEM(space_taps.shape, F32),
            pltpu.VMEM((1, fir_taps.shape[0]), BF16),
            pltpu.VMEM((rows, length), BF16),
            pltpu.VMEM((8, 2 * LANES), F32),
            pltpu.VMEM((rows, length), BF16),
            pltpu.VMEM((2 * half, length), BF16),
            pltpu.VMEM((half, length), BF16),
            pltpu.VMEM((half, length), BF16),
            pltpu.VMEM((chans, 2 * SLOT, LANES), BF16),
            pltpu.VMEM((rows, length), F32),
            pltpu.VMEM((2 * SLOT, length), F32),
            pltpu.SemaphoreType.DMA((4,)),
            pltpu.SemaphoreType.DMA,
            pltpu.SemaphoreType.DMA((2,)),
            pltpu.SemaphoreType.DMA,
            pltpu.SemaphoreType.DMA,
            pltpu.SemaphoreType.REGULAR,
            pltpu.SemaphoreType.REGULAR((chans,)),
        ],
        compiler_params=pltpu.CompilerParams(
            collective_id=0, has_side_effects=True, vmem_limit_bytes=24 * 2**20
        ),
        name="exchange",
    )(
        *(
            pltpu.with_memory_space_constraint(x, pltpu.HBM)
            for x in (source_index, space_taps, fir_taps.reshape(1, -1), raw_traces)
        )
    )
    if split:
        return pl.pallas_call(
            functools.partial(finish_kernel, per),
            out_shape=jax.ShapeDtypeStruct((rows, LAGS, total), BF16),
            in_specs=[vmem] * 4,
            out_specs=pl.BlockSpec(memory_space=pl.ANY),
            scratch_shapes=[
                pltpu.VMEM((2 * LANES, length), BF16),
                pltpu.VMEM(blocks.shape, BF16),
                pltpu.SemaphoreType.DMA((LAGS // MINOR,)),
            ],
            compiler_params=pltpu.CompilerParams(vmem_limit_bytes=40 * 2**20),
            name="finish",
        )(gathered, far, shifted, *early)
    return pl.pallas_call(
        functools.partial(correlate_kernel, per),
        out_shape=jax.ShapeDtypeStruct((rows, LAGS, total), BF16),
        in_specs=[vmem, vmem, vmem],
        out_specs=pl.BlockSpec(memory_space=pl.ANY),
        scratch_shapes=[
            pltpu.VMEM((steps, 2 * lanes, length), BF16),
            pltpu.VMEM((steps, rows, 2 * MINOR, total), BF16),
            pltpu.SemaphoreType.DMA((steps,)),
        ],
        compiler_params=pltpu.CompilerParams(vmem_limit_bytes=40 * 2**20),
        name="correlate",
    )(gathered, far, shifted)


def solution(mesh):
    return jax.shard_map(
        functools.partial(shards, mesh.shape["section"], mesh.shape["chan"]),
        mesh=mesh,
        in_specs=(P(("section", "chan"), None), P(), P(), P("section", "chan")),
        out_specs=P(("section", "chan"), None, None),
        check_vma=False,
    )
```

```python
import functools

import jax
import jax.numpy as jnp
from jax import lax
from jax.experimental import pallas as pl
from jax.experimental.pallas import tpu as pltpu
from jax.sharding import PartitionSpec as P

LAGS = 64
MINOR = 16
SLOT = 8
LANES = 128
MESH = pl.DeviceIdType.MESH
F32, BF16 = jnp.float32, jnp.bfloat16


def iota(shape, dim):
    return lax.broadcasted_iota(jnp.int32, shape, dim)


def dot(a, b, contract=((1,), (0,))):
    return lax.dot_general(a, b, (contract, ((), ())), preferred_element_type=F32)


def fir_block(fir_ref, line_ref):
    taps = fir_ref.shape[1]
    line_ref[...] = jnp.zeros(line_ref.shape, F32)
    line_ref[0:1, 0:taps] = fir_ref[...].astype(F32)
    wide = jnp.broadcast_to(line_ref[0:1, 0 : 2 * LANES], (2 * LANES, 2 * LANES))
    toeplitz = pltpu.roll(wide, LANES, 1, stride=1, stride_axis=0)[:, :LANES]
    flip = (iota((LANES, LANES), 0) + iota((LANES, LANES), 1) == LANES - 1).astype(F32)
    return dot(toeplitz.astype(BF16), flip.astype(BF16)).astype(BF16)


def fir(x, block):
    rows, length = x.shape
    count = length // LANES
    parts = []
    for b in range(count):
        now = x[:, b * LANES : (b + 1) * LANES]
        before = x[:, (b - 1) * LANES : b * LANES] if b else jnp.zeros_like(now)
        parts.append(jnp.concatenate([before, now], axis=1))
    y = dot(jnp.concatenate(parts, axis=0), block).astype(BF16)
    return [y[b * rows : (b + 1) * rows] for b in reversed(range(count))]


def split3(x):
    high = x.astype(BF16)
    rest = x - high.astype(F32)
    middle = rest.astype(BF16)
    low = (rest - middle.astype(F32)).astype(BF16)
    return high, middle, low


def unpack(gathered_ref, begin, number, length):
    middle = length // 2
    upper = iota((SLOT, middle), 0) < SLOT // 2
    parts = []
    for j in range(0, number, 2):
        a, b = (gathered_ref[begin + j + i].astype(F32) for i in range(2))
        tail_a, tail_b = a[:, length:], b[:, length:]
        turn_a, turn_b = (pltpu.roll(x, SLOT // 2, 0) for x in (tail_a, tail_b))
        shared = [jnp.where(upper, tail_a, turn_b), jnp.where(upper, turn_a, tail_b)]
        parts += [a[:, :length], jnp.concatenate(shared, axis=1), b[:, :length]]
    return parts


def place(high, gathered_ref, far_ref):
    length = far_ref.shape[1]
    part = gathered_ref.shape[0] // 2
    parts = unpack(gathered_ref, jnp.where(high, part, 0), part, length)
    for i in range(2):
        parts[i - 2] += jnp.where(high, far_ref[i * SLOT : (i + 1) * SLOT], 0.0)
    scale = 1.0 / length**0.5
    even = [x * scale for x in parts]
    odd = [advance(x, MINOR) for x in even]
    count, half = len(even), LANES // 2 // SLOT
    zero = jnp.zeros((SLOT, length), F32)
    wide = [zero] * (2 * half)
    low, up = list(wide), list(wide)
    for i in range(count):
        low[i], low[half + i] = even[i], odd[i]
        up[count + i], up[(count + half + i) % (2 * half)] = even[i], odd[i]
    chosen = []
    for a, b in zip(low, up):
        chosen.append(jnp.where(high, b, a))
    return jnp.concatenate(chosen, axis=0)


def advance(x, shift):
    if not shift:
        return x
    length = x.shape[1]
    moved = pltpu.roll(x, length - shift, 1)
    edge = iota((x.shape[0], LANES), 1)
    tail = jnp.where(edge < LANES - shift, moved[:, length - LANES :], 0.0)
    return jnp.concatenate([moved[:, : length - LANES], tail], axis=1)


def correlate(per, high, gathered_ref, far_ref, shifted_ref, weights, blocks, given, finish=None):
    length = shifted_ref.shape[1]
    rows = shifted_ref.shape[0] // MINOR
    chans = gathered_ref.shape[0]
    total = per * chans
    sources = place(high, gathered_ref, far_ref)
    lane = iota((rows, MINOR, total), 2) - jnp.where(high, total // 2, 0)
    keep = jnp.logical_and(lane >= 0, lane < total // 2)
    for h in range(2):
        moved = advance(sources, h * 2 * MINOR)
        weights[h * LANES : (h + 1) * LANES, :] = moved.astype(BF16)
    result = dot(shifted_ref[...], weights[...], ((1,), (1,)))
    for h in range(2):
        pair = result[:, h * LANES : (h + 1) * LANES]
        for i in range(2):
            turned = pltpu.roll(pair, LANES // 2, 1) if i else pair
            block = turned.reshape(rows, MINOR, LANES)[:, :, :total].astype(BF16)
            k = 2 * h + i
            blocks[k] = block if given is None else jnp.where(keep, block, given[k])
            if finish:
                finish(k)


def exchange_kernel(
    sections, chans, per,
    index_hbm, space_hbm, fir_hbm, raw_hbm,
    gathered_ref, far_ref, shifted_ref, *rest,
):
    (
        *early, weights, index_ref, space_ref, fir_ref, raw_ref, line, band,
        halo, above_raw, far_rows, slope, own_ref, source_ref,
        local_sem, edge_sem, recv_sem, far_sem, slope_sem, seen, far_seen,
    ) = rest
    rows, length = raw_ref.shape
    half = halo.shape[0] // 2
    sec, ch = lax.axis_index("section"), lax.axis_index("chan")
    me = sec * chans + ch
    above = sec < sections - 1
    first, final = ch == 0, ch == chans - 1
    serves = jnp.logical_and(first, sec > 0)
    served = jnp.logical_and(final, above)
    below = jnp.maximum(sec - 1, 0)
    above_id = (jnp.minimum(sec + 1, sections - 1), 0)
    prev_id = (sec, jnp.maximum(ch - 1, 0))
    next_id = (sec, jnp.minimum(ch + 1, chans - 1))

    load_raw = pltpu.make_async_copy(raw_hbm, raw_ref, local_sem.at[0])
    load_fir = pltpu.make_async_copy(fir_hbm, fir_ref, local_sem.at[1])
    load_space = pltpu.make_async_copy(space_hbm, space_ref, local_sem.at[2])
    load_index = pltpu.make_async_copy(index_hbm, index_ref, local_sem.at[3])
    def signal(sem, device):
        pl.semaphore_signal(sem, inc=1, device_id=device, device_id_type=MESH)

    def remote(src, dst, send, recv, device):
        return pltpu.make_async_remote_copy(
            src_ref=src, dst_ref=dst, send_sem=send, recv_sem=recv,
            device_id=device, device_id_type=MESH,
        )

    barrier = pltpu.get_barrier_semaphore()

    @pl.when(ch > 0)
    def _():
        signal(barrier, prev_id)

    load_fir.start()
    load_raw.start()
    load_space.start()
    load_index.start()

    for c in range(1, chans):
        @pl.when(c > ch)
        def _():
            signal(barrier, (sec, c))

    @pl.when(serves)
    def _():
        for c in range(chans - 1, 0, -1):
            signal(barrier, (below, c))

    @pl.when(jnp.logical_and(first, above))
    def _():
        signal(barrier, above_id)

    edge_send, packet_send, far_send, slope_send = (local_sem.at[i] for i in range(4))
    to_prev = remote(
        band.at[0:half], halo.at[half : 2 * half], edge_send, edge_sem, prev_id
    )
    to_next = remote(
        band.at[rows - half : rows], halo.at[0:half], edge_send, edge_sem, next_id
    )
    to_above = remote(
        raw_ref.at[rows - half : rows], above_raw, edge_send, edge_sem, above_id
    )
    edges_two = remote(halo, halo, edge_send, edge_sem, next_id)
    edges_one = remote(halo.at[0:half], halo.at[0:half], edge_send, edge_sem, next_id)

    def to_below(c):
        return remote(
            band.at[0:half], far_rows, far_send, far_sem, (below, c)
        )

    def slope_to(c):
        return remote(slope.at[chans - 1], slope.at[chans - 1], slope_send, slope_sem, (sec, c))

    def enter():
        pl.semaphore_wait(
            barrier,
            ch
            + (ch < chans - 1).astype(jnp.int32)
            + jnp.logical_and(ch > 0, above).astype(jnp.int32)
            + jnp.logical_and(first, sec > 0).astype(jnp.int32),
        )

        @pl.when(jnp.logical_and(ch > 0, above))
        def _():
            signal(far_seen.at[ch // 2], above_id)

        for c in range(chans - 2):
            @pl.when(c < ch - 1)
            def _():
                signal(seen, (sec, c))

    pl.when(final)(enter)

    load_fir.wait()
    block = fir_block(fir_ref, line)
    load_raw.wait()
    for b, part in enumerate(fir(raw_ref[...], block)):
        band[:, b * LANES : (b + 1) * LANES] = part

    pl.when(jnp.logical_not(final))(enter)

    @pl.when(jnp.logical_not(final))
    def _():
        to_next.start()

    @pl.when(ch > 0)
    def _():
        to_prev.start()

    @pl.when(served)
    def _():
        to_above.start()

    load_space.wait()
    load_index.wait()
    taps = space_ref.shape[0]

    def mixing(width, place):
        offset = place(iota((rows, width), 1)) - iota((rows, width), 0)
        mix = jnp.zeros((rows, width), F32)
        for j in range(taps):
            mix = jnp.where(offset == j, space_ref[j], mix)
        return jnp.concatenate(split3(mix), axis=1)

    mix_own = mixing(rows, lambda col: col + half)
    mix_halo = mixing(2 * half, lambda col: jnp.where(col < half, col, col + rows))
    mix_right = mixing(half, lambda col: col + half + rows)
    count = index_ref.shape[1]
    row, col = iota((2 * SLOT, rows), 0), iota((2 * SLOT, rows), 1)
    pick = jnp.zeros((2 * SLOT, rows), F32)
    odd = jnp.bitwise_and(ch, 1)
    extra = count - SLOT
    for i in range(2 * SLOT):
        which = i + extra * odd if i < SLOT else (i - SLOT) % extra + SLOT * (1 - odd)
        source = index_ref[0, which] - ch * rows
        pick = jnp.where(jnp.logical_and(row == i, col == source), 1.0, pick)
    pick = pick.astype(BF16)
    source_own = dot(pick, mix_own).astype(BF16)
    source_halo = dot(pick, mix_halo).astype(BF16)

    def thrice(x):
        return jnp.concatenate([x] * 3, axis=0)

    @pl.when(served)
    def _():
        late = jnp.zeros((2 * SLOT, rows), F32)
        for i in range(count):
            source = index_ref[0, i] - ch * rows
            chosen = jnp.logical_and(row == i + 2 * SLOT - count, col == source)
            late = jnp.where(chosen, 1.0, late)
        slope[chans - 1, :, 0 : 3 * half] = dot(late.astype(BF16), mix_right).astype(BF16)

    whole = thrice(band[...])
    own_ref[...] = dot(mix_own, whole)
    source_ref[...] = dot(source_own, whole)

    @pl.when(served)
    def _():
        for c in range(chans - 1):
            slope_to(c).start()

    @pl.when(serves)
    def _():
        for c in range(chans):
            if c == 1:
                pl.semaphore_wait(far_seen.at[0], 1)
            elif c and c % 2 == 0:
                pl.semaphore_wait(far_seen.at[c // 2], 2)
            to_below(c).start()

    @pl.when(final)
    def _():
        halo[half : 2 * half] = jnp.zeros((half, length), BF16)

    single = jnp.logical_or(final, me == 0)

    @pl.when(jnp.logical_not(single))
    def _():
        edges_two.wait_recv()

    @pl.when(single)
    def _():
        edges_one.wait_recv()

    @pl.when(serves)
    def _():
        for b, part in enumerate(fir(above_raw[...], block)):
            halo[0:half, b * LANES : (b + 1) * LANES] = part

    @pl.when(me == 0)
    def _():
        halo[0:half] = jnp.zeros((half, length), BF16)

    edges = thrice(halo[...])
    sources = source_ref[...] + dot(source_halo, edges)
    middle = length // 2
    tail = jnp.where(
        iota((SLOT, middle), 0) < SLOT // 2,
        sources[SLOT : 2 * SLOT, 0:middle], sources[SLOT : 2 * SLOT, middle:length],
    )
    gathered_ref[ch] = jnp.concatenate([sources[0:SLOT], tail], axis=1).astype(BF16)

    part = chans // 2

    def packet(source, c):
        return remote(
            gathered_ref.at[source], gathered_ref.at[source],
            packet_send, recv_sem.at[((c < part) ^ (source < part)).astype(jnp.int32)], (sec, c),
        )

    for c in range(2):
        @pl.when(c < ch)
        def _():
            packet(ch, c).start()

    @pl.when(ch < chans - 2)
    def _():
        pl.semaphore_wait(seen, chans - 2 - ch)

    for c in range(1, chans):
        @pl.when(c > ch)
        def _():
            packet(ch, c).start()

    for c in range(chans - 2, 1, -1):
        @pl.when(c < ch)
        def _():
            packet(ch, c).start()

    own_ref[...] += dot(mix_halo, edges)

    @pl.when(served)
    def _():
        to_below(0).wait_recv()
        own_ref[...] += dot(mix_right, thrice(far_rows[...]))

    own_ref[...] = own_ref[...].astype(BF16).astype(F32)
    keep = iota((MINOR, length), 1) >= iota((MINOR, length), 0)
    for c in range(rows):
        wide = jnp.broadcast_to(own_ref[c : c + 1, :], (MINOR, length))
        wide = pltpu.roll(wide, 0, 1, stride=1, stride_axis=0)
        shifted_ref[c * MINOR : (c + 1) * MINOR, :] = jnp.where(keep, wide, 0.0).astype(BF16)

    @pl.when(jnp.logical_and(above, jnp.logical_not(final)))
    def _():
        to_below(0).wait_recv()
        slope_to(0).wait_recv()

    @pl.when(above)
    def _():
        far_ref[...] = dot(slope[chans - 1, :, 0 : 3 * half], thrice(far_rows[...]))

    @pl.when(jnp.logical_not(above))
    def _():
        far_ref[...] = jnp.zeros(far_ref.shape, F32)

    near = gathered_ref.at[0 : part - 1]
    remote(near, near, packet_send, recv_sem.at[0], next_id).wait_recv()
    if early:
        correlate(per, ch >= part, gathered_ref, far_ref, shifted_ref, weights, early[0], None)
    alone = jnp.logical_or(first, jnp.logical_and(final, jnp.logical_not(above)))

    @pl.when(jnp.logical_not(alone))
    def _():
        edges_two.wait_send()

    @pl.when(alone)
    def _():
        edges_one.wait_send()

    @pl.when(served)
    def _():
        every = slope.at[0 : chans - 1]
        remote(every, every, slope_send, slope_sem, prev_id).wait_send()

    @pl.when(serves)
    def _():
        every = shifted_ref.at[0 : chans * half]
        remote(every, every, far_send, far_sem, next_id).wait_send()

    every = gathered_ref.at[0 : chans - 1]
    remote(every, every, packet_send, recv_sem.at[0], next_id).wait_send()
    away = gathered_ref.at[0:part]
    remote(away, away, packet_send, recv_sem.at[1], next_id).wait_recv()


def correlate_kernel(per, gathered_ref, far_ref, shifted_ref, out_ref, weights, blocks, sems):
    chans = gathered_ref.shape[0]
    length = shifted_ref.shape[1]
    rows, lags, total = out_ref.shape
    lanes = pl.cdiv(total, LANES) * LANES
    sources = jnp.concatenate(unpack(gathered_ref, 0, chans, length), axis=0)
    edge = iota((total, LANES), 1)
    top = total - 2 * SLOT
    sources = jnp.concatenate([sources[:top], sources[top:] + far_ref[...]], axis=0)
    scale = 1.0 / length**0.5
    if lanes > total:
        for h in range(2):
            fill = jnp.zeros((weights.shape[0], lanes - total, length), BF16)
            weights[:, h * lanes + total : (h + 1) * lanes, :] = fill
    copies = []
    for k in range(lags // (2 * MINOR)):
        for h in range(2):
            shift = (2 * k + h) * MINOR
            moved = sources
            if shift:
                moved = pltpu.roll(sources, length - shift, 1)
                tail = jnp.where(edge < LANES - shift, moved[:, length - LANES :], 0.0)
                moved = jnp.concatenate([moved[:, : length - LANES], tail], axis=1)
            weights[k, h * lanes : h * lanes + total, :] = moved.astype(BF16)
        result = dot(shifted_ref[...], weights[k], ((1,), (1,))) * scale
        low = result[:, 0:total].reshape(rows, MINOR, total)
        high = result[:, lanes : lanes + total].reshape(rows, MINOR, total)
        blocks[k] = jnp.concatenate([low, high], axis=1).astype(BF16)
        copy = pltpu.make_async_copy(
            blocks.at[k], out_ref.at[:, k * 2 * MINOR : (k + 1) * 2 * MINOR, :], sems.at[k]
        )
        copy.start()
        copies.append(copy)
    for copy in copies:
        copy.wait()


def finish_kernel(per, gathered_ref, far_ref, shifted_ref, early_ref, out_ref, weights, blocks, sems):
    chans = gathered_ref.shape[0]
    depth = blocks.shape[2]

    def out(k):
        return pltpu.make_async_copy(
            blocks.at[k], out_ref.at[:, k * depth : (k + 1) * depth, :], sems.at[k]
        )

    high = lax.axis_index("chan") < chans // 2
    correlate(
        per, high, gathered_ref, far_ref, shifted_ref, weights, blocks, early_ref,
        lambda k: out(k).start(),
    )
    for k in range(blocks.shape[0]):
        out(k).wait()


def shards(sections, chans, raw_traces, fir_taps, space_taps, source_index):
    rows, length = raw_traces.shape
    half = (space_taps.shape[0] - 1) // 2
    per = source_index.shape[1]
    total = per * chans
    lanes = -(-total // LANES) * LANES
    steps = LAGS // (2 * MINOR)
    vmem, hbm = pl.BlockSpec(memory_space=pltpu.VMEM), pl.BlockSpec(memory_space=pltpu.HBM)
    split = total <= LANES
    blocks = jax.ShapeDtypeStruct((LAGS // MINOR, rows, MINOR, total), BF16)
    gathered, far, shifted, *early = pl.pallas_call(
        functools.partial(exchange_kernel, sections, chans, per),
        out_shape=(
            jax.ShapeDtypeStruct((chans, SLOT, length + length // 2), BF16),
            jax.ShapeDtypeStruct((2 * SLOT, length), F32),
            jax.ShapeDtypeStruct((rows * MINOR, length), BF16),
            *([blocks] if split else []),
        ),
        in_specs=[hbm, hbm, hbm, hbm],
        out_specs=(vmem,) * (4 if split else 3),
        scratch_shapes=[
            pltpu.VMEM((2 * LANES, length), BF16),
            pltpu.SMEM(source_index.shape, jnp.int32),
            pltpu.SMEM(space_taps.shape, F32),
            pltpu.VMEM((1, fir_taps.shape[0]), BF16),
            pltpu.VMEM((rows, length), BF16),
            pltpu.VMEM((8, 2 * LANES), F32),
            pltpu.VMEM((rows, length), BF16),
            pltpu.VMEM((2 * half, length), BF16),
            pltpu.VMEM((half, length), BF16),
            pltpu.VMEM((half, length), BF16),
            pltpu.VMEM((chans, 2 * SLOT, LANES), BF16),
            pltpu.VMEM((rows, length), F32),
            pltpu.VMEM((2 * SLOT, length), F32),
            pltpu.SemaphoreType.DMA((4,)),
            pltpu.SemaphoreType.DMA,
            pltpu.SemaphoreType.DMA((2,)),
            pltpu.SemaphoreType.DMA,
            pltpu.SemaphoreType.DMA,
            pltpu.SemaphoreType.REGULAR,
            pltpu.SemaphoreType.REGULAR((chans // 2,)),
        ],
        compiler_params=pltpu.CompilerParams(
            collective_id=0, has_side_effects=True, vmem_limit_bytes=24 * 2**20
        ),
        name="exchange",
    )(
        *(
            pltpu.with_memory_space_constraint(x, pltpu.HBM)
            for x in (source_index, space_taps, fir_taps.reshape(1, -1), raw_traces)
        )
    )
    if split:
        return pl.pallas_call(
            functools.partial(finish_kernel, per),
            out_shape=jax.ShapeDtypeStruct((rows, LAGS, total), BF16),
            in_specs=[vmem] * 4,
            out_specs=pl.BlockSpec(memory_space=pl.ANY),
            scratch_shapes=[
                pltpu.VMEM((2 * LANES, length), BF16),
                pltpu.VMEM(blocks.shape, BF16),
                pltpu.SemaphoreType.DMA((LAGS // MINOR,)),
            ],
            compiler_params=pltpu.CompilerParams(vmem_limit_bytes=40 * 2**20),
            name="finish",
        )(gathered, far, shifted, *early)
    return pl.pallas_call(
        functools.partial(correlate_kernel, per),
        out_shape=jax.ShapeDtypeStruct((rows, LAGS, total), BF16),
        in_specs=[vmem, vmem, vmem],
        out_specs=pl.BlockSpec(memory_space=pl.ANY),
        scratch_shapes=[
            pltpu.VMEM((steps, 2 * lanes, length), BF16),
            pltpu.VMEM((steps, rows, 2 * MINOR, total), BF16),
            pltpu.SemaphoreType.DMA((steps,)),
        ],
        compiler_params=pltpu.CompilerParams(vmem_limit_bytes=40 * 2**20),
        name="correlate",
    )(gathered, far, shifted)


def solution(mesh):
    return jax.shard_map(
        functools.partial(shards, mesh.shape["section"], mesh.shape["chan"]),
        mesh=mesh,
        in_specs=(P(("section", "chan"), None), P(), P(), P("section", "chan")),
        out_specs=P(("section", "chan"), None, None),
        check_vma=False,
    )
```

```python
import functools

import jax
import jax.numpy as jnp
from jax import lax
from jax.experimental import pallas as pl
from jax.experimental.pallas import tpu as pltpu
from jax.sharding import PartitionSpec as P

LAGS = 64
MINOR = 16
SLOT = 8
LANES = 128
MESH = pl.DeviceIdType.MESH
F32, BF16 = jnp.float32, jnp.bfloat16


def iota(shape, dim):
    return lax.broadcasted_iota(jnp.int32, shape, dim)


def dot(a, b, contract=((1,), (0,))):
    return lax.dot_general(a, b, (contract, ((), ())), preferred_element_type=F32)


def fir_block(fir_ref, line_ref):
    taps = fir_ref.shape[1]
    line_ref[...] = jnp.zeros(line_ref.shape, F32)
    line_ref[0:1, 0:taps] = fir_ref[...].astype(F32)
    wide = jnp.broadcast_to(line_ref[0:1, 0 : 2 * LANES], (2 * LANES, 2 * LANES))
    toeplitz = pltpu.roll(wide, LANES, 1, stride=1, stride_axis=0)[:, :LANES]
    flip = (iota((LANES, LANES), 0) + iota((LANES, LANES), 1) == LANES - 1).astype(F32)
    return dot(toeplitz.astype(BF16), flip.astype(BF16)).astype(BF16)


def fir(x, block):
    rows, length = x.shape
    count = length // LANES
    parts = []
    for b in range(count):
        now = x[:, b * LANES : (b + 1) * LANES]
        before = x[:, (b - 1) * LANES : b * LANES] if b else jnp.zeros_like(now)
        parts.append(jnp.concatenate([before, now], axis=1))
    y = dot(jnp.concatenate(parts, axis=0), block).astype(BF16)
    return [y[b * rows : (b + 1) * rows] for b in reversed(range(count))]


def split3(x):
    high = x.astype(BF16)
    rest = x - high.astype(F32)
    middle = rest.astype(BF16)
    low = (rest - middle.astype(F32)).astype(BF16)
    return high, middle, low


def unpack(gathered_ref, begin, number, length):
    middle = length // 2
    upper = iota((SLOT, middle), 0) < SLOT // 2
    parts = []
    for j in range(0, number, 2):
        a, b = (gathered_ref[begin + j + i].astype(F32) for i in range(2))
        tail_a, tail_b = a[:, length:], b[:, length:]
        turn_a, turn_b = (pltpu.roll(x, SLOT // 2, 0) for x in (tail_a, tail_b))
        shared = [jnp.where(upper, tail_a, turn_b), jnp.where(upper, turn_a, tail_b)]
        parts += [a[:, :length], jnp.concatenate(shared, axis=1), b[:, :length]]
    return parts


def place(high, gathered_ref, far_ref):
    length = far_ref.shape[1]
    part = gathered_ref.shape[0] // 2
    parts = unpack(gathered_ref, jnp.where(high, part, 0), part, length)
    for i in range(2):
        parts[i - 2] += jnp.where(high, far_ref[i * SLOT : (i + 1) * SLOT], 0.0)
    scale = 1.0 / length**0.5
    even = [x * scale for x in parts]
    odd = [advance(x, MINOR) for x in even]
    count, half = len(even), LANES // 2 // SLOT
    zero = jnp.zeros((SLOT, length), F32)
    wide = [zero] * (2 * half)
    low, up = list(wide), list(wide)
    for i in range(count):
        low[i], low[half + i] = even[i], odd[i]
        up[count + i], up[(count + half + i) % (2 * half)] = even[i], odd[i]
    chosen = []
    for a, b in zip(low, up):
        chosen.append(jnp.where(high, b, a))
    return jnp.concatenate(chosen, axis=0)


def advance(x, shift):
    if not shift:
        return x
    length = x.shape[1]
    moved = pltpu.roll(x, length - shift, 1)
    edge = iota((x.shape[0], LANES), 1)
    tail = jnp.where(edge < LANES - shift, moved[:, length - LANES :], 0.0)
    return jnp.concatenate([moved[:, : length - LANES], tail], axis=1)


def correlate(per, high, gathered_ref, far_ref, shifted_ref, weights, blocks, given, finish=None):
    length = shifted_ref.shape[1]
    rows = shifted_ref.shape[0] // MINOR
    chans = gathered_ref.shape[0]
    total = per * chans
    sources = place(high, gathered_ref, far_ref)
    lane = iota((rows, MINOR, total), 2) - jnp.where(high, total // 2, 0)
    keep = jnp.logical_and(lane >= 0, lane < total // 2)
    for h in range(2):
        moved = advance(sources, h * 2 * MINOR)
        weights[h * LANES : (h + 1) * LANES, :] = moved.astype(BF16)
    result = dot(shifted_ref[...], weights[...], ((1,), (1,)))
    for h in range(2):
        pair = result[:, h * LANES : (h + 1) * LANES]
        for i in range(2):
            turned = pltpu.roll(pair, LANES // 2, 1) if i else pair
            block = turned.reshape(rows, MINOR, LANES)[:, :, :total].astype(BF16)
            k = 2 * h + i
            blocks[k] = block if given is None else jnp.where(keep, block, given[k])
            if finish:
                finish(k)


def exchange_kernel(
    sections, chans, per,
    index_hbm, space_hbm, fir_hbm, raw_hbm,
    gathered_ref, far_ref, shifted_ref, *rest,
):
    (
        *early, weights, index_ref, space_ref, fir_ref, raw_ref, line, band,
        halo, above_raw, far_rows, slope, own_ref, source_ref,
        local_sem, edge_sem, recv_sem, far_sem, slope_sem, seen, far_seen,
    ) = rest
    rows, length = raw_ref.shape
    half = halo.shape[0] // 2
    sec, ch = lax.axis_index("section"), lax.axis_index("chan")
    me = sec * chans + ch
    above = sec < sections - 1
    first, final = ch == 0, ch == chans - 1
    serves = jnp.logical_and(first, sec > 0)
    served = jnp.logical_and(final, above)
    below = jnp.maximum(sec - 1, 0)
    above_id = (jnp.minimum(sec + 1, sections - 1), 0)
    prev_id = (sec, jnp.maximum(ch - 1, 0))
    next_id = (sec, jnp.minimum(ch + 1, chans - 1))

    load_raw = pltpu.make_async_copy(raw_hbm, raw_ref, local_sem.at[0])
    load_fir = pltpu.make_async_copy(fir_hbm, fir_ref, local_sem.at[1])
    load_space = pltpu.make_async_copy(space_hbm, space_ref, local_sem.at[2])
    load_index = pltpu.make_async_copy(index_hbm, index_ref, local_sem.at[3])
    def signal(sem, device):
        pl.semaphore_signal(sem, inc=1, device_id=device, device_id_type=MESH)

    def remote(src, dst, send, recv, device):
        return pltpu.make_async_remote_copy(
            src_ref=src, dst_ref=dst, send_sem=send, recv_sem=recv,
            device_id=device, device_id_type=MESH,
        )

    barrier = pltpu.get_barrier_semaphore()

    @pl.when(ch > 0)
    def _():
        signal(barrier, prev_id)

    load_fir.start()
    load_raw.start()
    load_space.start()
    load_index.start()

    for c in range(1, chans):
        @pl.when(c > ch)
        def _():
            signal(barrier, (sec, c))

    @pl.when(serves)
    def _():
        for c in range(chans - 1, 0, -1):
            signal(barrier, (below, c))

    @pl.when(jnp.logical_and(first, above))
    def _():
        signal(barrier, above_id)

    edge_send, packet_send, far_send, slope_send = (local_sem.at[i] for i in range(4))
    to_prev = remote(
        band.at[0:half], halo.at[half : 2 * half], edge_send, edge_sem, prev_id
    )
    to_next = remote(
        band.at[rows - half : rows], halo.at[0:half], edge_send, edge_sem, next_id
    )
    to_above = remote(
        raw_ref.at[rows - half : rows], above_raw, edge_send, edge_sem, above_id
    )
    edges_two = remote(halo, halo, edge_send, edge_sem, next_id)
    edges_one = remote(halo.at[0:half], halo.at[0:half], edge_send, edge_sem, next_id)

    def to_below(c):
        return remote(
            band.at[0:half], far_rows, far_send, far_sem, (below, c)
        )

    def slope_to(c):
        return remote(slope.at[chans - 1], slope.at[chans - 1], slope_send, slope_sem, (sec, c))

    def enter():
        pl.semaphore_wait(
            barrier,
            ch
            + (ch < chans - 1).astype(jnp.int32)
            + jnp.logical_and(ch > 0, above).astype(jnp.int32)
            + jnp.logical_and(first, sec > 0).astype(jnp.int32),
        )

        @pl.when(jnp.logical_and(ch > 0, above))
        def _():
            signal(far_seen.at[ch // 2], above_id)

        for c in range(chans - 2):
            @pl.when(c < ch - 1)
            def _():
                signal(seen, (sec, c))

    pl.when(final)(enter)

    load_fir.wait()
    block = fir_block(fir_ref, line)
    load_raw.wait()
    for b, part in enumerate(fir(raw_ref[...], block)):
        band[:, b * LANES : (b + 1) * LANES] = part

    pl.when(jnp.logical_not(final))(enter)

    @pl.when(jnp.logical_not(final))
    def _():
        to_next.start()

    @pl.when(ch > 0)
    def _():
        to_prev.start()

    @pl.when(served)
    def _():
        to_above.start()

    load_space.wait()
    load_index.wait()
    taps = space_ref.shape[0]

    def mixing(width, place):
        offset = place(iota((rows, width), 1)) - iota((rows, width), 0)
        mix = jnp.zeros((rows, width), F32)
        for j in range(taps):
            mix = jnp.where(offset == j, space_ref[j], mix)
        return jnp.concatenate(split3(mix), axis=1)

    mix_own = mixing(rows, lambda col: col + half)
    mix_halo = mixing(2 * half, lambda col: jnp.where(col < half, col, col + rows))
    mix_right = mixing(half, lambda col: col + half + rows)
    count = index_ref.shape[1]
    row, col = iota((2 * SLOT, rows), 0), iota((2 * SLOT, rows), 1)
    pick = jnp.zeros((2 * SLOT, rows), F32)
    odd = jnp.bitwise_and(ch, 1)
    extra = count - SLOT
    for i in range(2 * SLOT):
        which = i + extra * odd if i < SLOT else (i - SLOT) % extra + SLOT * (1 - odd)
        source = index_ref[0, which] - ch * rows
        pick = jnp.where(jnp.logical_and(row == i, col == source), 1.0, pick)
    pick = pick.astype(BF16)
    source_own = dot(pick, mix_own).astype(BF16)
    source_halo = dot(pick, mix_halo).astype(BF16)

    def thrice(x):
        return jnp.concatenate([x] * 3, axis=0)

    @pl.when(served)
    def _():
        late = jnp.zeros((2 * SLOT, rows), F32)
        for i in range(count):
            source = index_ref[0, i] - ch * rows
            chosen = jnp.logical_and(row == i + 2 * SLOT - count, col == source)
            late = jnp.where(chosen, 1.0, late)
        slope[chans - 1, :, 0 : 3 * half] = dot(late.astype(BF16), mix_right).astype(BF16)

    whole = thrice(band[...])
    own_ref[...] = dot(mix_own, whole)
    source_ref[...] = dot(source_own, whole)

    @pl.when(served)
    def _():
        for c in range(chans - 1):
            slope_to(c).start()

    @pl.when(serves)
    def _():
        for c in range(chans):
            if c == 1:
                pl.semaphore_wait(far_seen.at[0], 1)
            elif c and c % 2 == 0:
                pl.semaphore_wait(far_seen.at[c // 2], 2)
            to_below(c).start()

    @pl.when(final)
    def _():
        halo[half : 2 * half] = jnp.zeros((half, length), BF16)

    single = jnp.logical_or(final, me == 0)

    @pl.when(jnp.logical_not(single))
    def _():
        edges_two.wait_recv()

    @pl.when(single)
    def _():
        edges_one.wait_recv()

    @pl.when(serves)
    def _():
        for b, part in enumerate(fir(above_raw[...], block)):
            halo[0:half, b * LANES : (b + 1) * LANES] = part

    @pl.when(me == 0)
    def _():
        halo[0:half] = jnp.zeros((half, length), BF16)

    edges = thrice(halo[...])
    sources = source_ref[...] + dot(source_halo, edges)
    middle = length // 2
    tail = jnp.where(
        iota((SLOT, middle), 0) < SLOT // 2,
        sources[SLOT : 2 * SLOT, 0:middle], sources[SLOT : 2 * SLOT, middle:length],
    )
    gathered_ref[ch] = jnp.concatenate([sources[0:SLOT], tail], axis=1).astype(BF16)

    part = chans // 2

    def packet(source, c):
        return remote(
            gathered_ref.at[source], gathered_ref.at[source],
            packet_send, recv_sem.at[((c < part) ^ (source < part)).astype(jnp.int32)], (sec, c),
        )

    for c in range(2):
        @pl.when(c < ch)
        def _():
            packet(ch, c).start()

    @pl.when(ch < chans - 2)
    def _():
        pl.semaphore_wait(seen, chans - 2 - ch)

    for c in range(1, chans):
        @pl.when(c > ch)
        def _():
            packet(ch, c).start()

    for c in [*range(chans - 2, 3, -1), 2, 3]:
        @pl.when(c < ch)
        def _():
            packet(ch, c).start()

    own_ref[...] += dot(mix_halo, edges)

    @pl.when(served)
    def _():
        to_below(0).wait_recv()
        own_ref[...] += dot(mix_right, thrice(far_rows[...]))

    own_ref[...] = own_ref[...].astype(BF16).astype(F32)
    keep = iota((MINOR, length), 1) >= iota((MINOR, length), 0)
    for c in range(rows):
        wide = jnp.broadcast_to(own_ref[c : c + 1, :], (MINOR, length))
        wide = pltpu.roll(wide, 0, 1, stride=1, stride_axis=0)
        shifted_ref[c * MINOR : (c + 1) * MINOR, :] = jnp.where(keep, wide, 0.0).astype(BF16)

    @pl.when(jnp.logical_and(above, jnp.logical_not(final)))
    def _():
        to_below(0).wait_recv()
        slope_to(0).wait_recv()

    @pl.when(above)
    def _():
        far_ref[...] = dot(slope[chans - 1, :, 0 : 3 * half], thrice(far_rows[...]))

    @pl.when(jnp.logical_not(above))
    def _():
        far_ref[...] = jnp.zeros(far_ref.shape, F32)

    near = gathered_ref.at[0 : part - 1]
    remote(near, near, packet_send, recv_sem.at[0], next_id).wait_recv()
    if early:
        correlate(per, ch >= part, gathered_ref, far_ref, shifted_ref, weights, early[0], None)
    alone = jnp.logical_or(first, jnp.logical_and(final, jnp.logical_not(above)))

    @pl.when(jnp.logical_not(alone))
    def _():
        edges_two.wait_send()

    @pl.when(alone)
    def _():
        edges_one.wait_send()

    @pl.when(served)
    def _():
        every = slope.at[0 : chans - 1]
        remote(every, every, slope_send, slope_sem, prev_id).wait_send()

    @pl.when(serves)
    def _():
        every = shifted_ref.at[0 : chans * half]
        remote(every, every, far_send, far_sem, next_id).wait_send()

    every = gathered_ref.at[0 : chans - 1]
    remote(every, every, packet_send, recv_sem.at[0], next_id).wait_send()
    away = gathered_ref.at[0:part]
    remote(away, away, packet_send, recv_sem.at[1], next_id).wait_recv()


def correlate_kernel(per, gathered_ref, far_ref, shifted_ref, out_ref, weights, blocks, sems):
    chans = gathered_ref.shape[0]
    length = shifted_ref.shape[1]
    rows, lags, total = out_ref.shape
    lanes = pl.cdiv(total, LANES) * LANES
    sources = jnp.concatenate(unpack(gathered_ref, 0, chans, length), axis=0)
    edge = iota((total, LANES), 1)
    top = total - 2 * SLOT
    sources = jnp.concatenate([sources[:top], sources[top:] + far_ref[...]], axis=0)
    scale = 1.0 / length**0.5
    if lanes > total:
        for h in range(2):
            fill = jnp.zeros((weights.shape[0], lanes - total, length), BF16)
            weights[:, h * lanes + total : (h + 1) * lanes, :] = fill
    copies = []
    for k in range(lags // (2 * MINOR)):
        for h in range(2):
            shift = (2 * k + h) * MINOR
            moved = sources
            if shift:
                moved = pltpu.roll(sources, length - shift, 1)
                tail = jnp.where(edge < LANES - shift, moved[:, length - LANES :], 0.0)
                moved = jnp.concatenate([moved[:, : length - LANES], tail], axis=1)
            weights[k, h * lanes : h * lanes + total, :] = moved.astype(BF16)
        result = dot(shifted_ref[...], weights[k], ((1,), (1,))) * scale
        low = result[:, 0:total].reshape(rows, MINOR, total)
        high = result[:, lanes : lanes + total].reshape(rows, MINOR, total)
        blocks[k] = jnp.concatenate([low, high], axis=1).astype(BF16)
        copy = pltpu.make_async_copy(
            blocks.at[k], out_ref.at[:, k * 2 * MINOR : (k + 1) * 2 * MINOR, :], sems.at[k]
        )
        copy.start()
        copies.append(copy)
    for copy in copies:
        copy.wait()


def finish_kernel(per, gathered_ref, far_ref, shifted_ref, early_ref, out_ref, weights, blocks, sems):
    chans = gathered_ref.shape[0]
    depth = blocks.shape[2]

    def out(k):
        return pltpu.make_async_copy(
            blocks.at[k], out_ref.at[:, k * depth : (k + 1) * depth, :], sems.at[k]
        )

    high = lax.axis_index("chan") < chans // 2
    correlate(
        per, high, gathered_ref, far_ref, shifted_ref, weights, blocks, early_ref,
        lambda k: out(k).start(),
    )
    for k in range(blocks.shape[0]):
        out(k).wait()


def shards(sections, chans, raw_traces, fir_taps, space_taps, source_index):
    rows, length = raw_traces.shape
    half = (space_taps.shape[0] - 1) // 2
    per = source_index.shape[1]
    total = per * chans
    lanes = -(-total // LANES) * LANES
    steps = LAGS // (2 * MINOR)
    vmem, hbm = pl.BlockSpec(memory_space=pltpu.VMEM), pl.BlockSpec(memory_space=pltpu.HBM)
    split = total <= LANES
    blocks = jax.ShapeDtypeStruct((LAGS // MINOR, rows, MINOR, total), BF16)
    gathered, far, shifted, *early = pl.pallas_call(
        functools.partial(exchange_kernel, sections, chans, per),
        out_shape=(
            jax.ShapeDtypeStruct((chans, SLOT, length + length // 2), BF16),
            jax.ShapeDtypeStruct((2 * SLOT, length), F32),
            jax.ShapeDtypeStruct((rows * MINOR, length), BF16),
            *([blocks] if split else []),
        ),
        in_specs=[hbm, hbm, hbm, hbm],
        out_specs=(vmem,) * (4 if split else 3),
        scratch_shapes=[
            pltpu.VMEM((2 * LANES, length), BF16),
            pltpu.SMEM(source_index.shape, jnp.int32),
            pltpu.SMEM(space_taps.shape, F32),
            pltpu.VMEM((1, fir_taps.shape[0]), BF16),
            pltpu.VMEM((rows, length), BF16),
            pltpu.VMEM((8, 2 * LANES), F32),
            pltpu.VMEM((rows, length), BF16),
            pltpu.VMEM((2 * half, length), BF16),
            pltpu.VMEM((half, length), BF16),
            pltpu.VMEM((half, length), BF16),
            pltpu.VMEM((chans, 2 * SLOT, LANES), BF16),
            pltpu.VMEM((rows, length), F32),
            pltpu.VMEM((2 * SLOT, length), F32),
            pltpu.SemaphoreType.DMA((4,)),
            pltpu.SemaphoreType.DMA,
            pltpu.SemaphoreType.DMA((2,)),
            pltpu.SemaphoreType.DMA,
            pltpu.SemaphoreType.DMA,
            pltpu.SemaphoreType.REGULAR,
            pltpu.SemaphoreType.REGULAR((chans // 2,)),
        ],
        compiler_params=pltpu.CompilerParams(
            collective_id=0, has_side_effects=True, vmem_limit_bytes=24 * 2**20
        ),
        name="exchange",
    )(
        *(
            pltpu.with_memory_space_constraint(x, pltpu.HBM)
            for x in (source_index, space_taps, fir_taps.reshape(1, -1), raw_traces)
        )
    )
    if split:
        return pl.pallas_call(
            functools.partial(finish_kernel, per),
            out_shape=jax.ShapeDtypeStruct((rows, LAGS, total), BF16),
            in_specs=[vmem] * 4,
            out_specs=pl.BlockSpec(memory_space=pl.ANY),
            scratch_shapes=[
                pltpu.VMEM((2 * LANES, length), BF16),
                pltpu.VMEM(blocks.shape, BF16),
                pltpu.SemaphoreType.DMA((LAGS // MINOR,)),
            ],
            compiler_params=pltpu.CompilerParams(vmem_limit_bytes=40 * 2**20),
            name="finish",
        )(gathered, far, shifted, *early)
    return pl.pallas_call(
        functools.partial(correlate_kernel, per),
        out_shape=jax.ShapeDtypeStruct((rows, LAGS, total), BF16),
        in_specs=[vmem, vmem, vmem],
        out_specs=pl.BlockSpec(memory_space=pl.ANY),
        scratch_shapes=[
            pltpu.VMEM((steps, 2 * lanes, length), BF16),
            pltpu.VMEM((steps, rows, 2 * MINOR, total), BF16),
            pltpu.SemaphoreType.DMA((steps,)),
        ],
        compiler_params=pltpu.CompilerParams(vmem_limit_bytes=40 * 2**20),
        name="correlate",
    )(gathered, far, shifted)


def solution(mesh):
    return jax.shard_map(
        functools.partial(shards, mesh.shape["section"], mesh.shape["chan"]),
        mesh=mesh,
        in_specs=(P(("section", "chan"), None), P(), P(), P("section", "chan")),
        out_specs=P(("section", "chan"), None, None),
        check_vma=False,
    )
```
